128 devices in a mesh: owner: 64 (over y, x, z), pair: 2 (over core).
Axes of the slice: x: 4, y: 4, z: 4, core: 2. Of those that a mesh axis runs over, the one named last changes fastest.
Arguments:
- incident: float32 [128, 2, 32, 512], P('owner', None, None, 'pair'), may hold values from -6 to 6
- tmat: float32 [128, 2, 512, 512], P('owner', None, 'pair'), may hold values from -0.1875 to 0.1875
- blocks: float32 [1344, 2, 512, 512], P('owner', None, None, 'pair'), may hold values from -0.09375 to 0.09375
- block_rows: int32 [1344], P('owner'), may hold values from 0 to 1
- partners: int32 [1344], replicated, may hold values from 0 to 127, as said below
- live: int32 [64], P('owner'), may hold values from 1 to 21, as said below
- owner_of: int32 [128], replicated, may hold values from 0 to 127, as said below
Outputs:
- scattered: float32 [128, 2, 32, 512], P('owner', None, None, 'pair')
- exciting: float32 [128, 2, 32, 512], P('owner', None, None, 'pair')
The draws below stay inside these ranges and needn't reach their ends.
Inputs may be any that keep to these rules, and one draw needn't show every extreme that they name: A permutation: particle p's coefficients and T-matrix stand in row owner_of[p]. `partners`: the 21 slots of one owner name distinct particles whose rows lie with owners either less than 8 positions away on either side around the cycle of owners or exactly 32 positions away, never the owner itself, at most 2 with any one other owner; for every owner some other owner holds exactly 2 of them. Slots n with n mod 21 below live[n // 21] are live; some owner has all 21 slots live.
All inputs are finite; a program needn't handle non-finite values.
Results may differ from the reference program's by a relative error of at most 0.0003.
Values sent between devices are 32-bit elements; how exact they have to be, the bound alone decides.
A program may use at most 128 MiB of HBM per device.

```python
import jax
import jax.numpy as jnp
from jax import lax

L = 512
K = 32
PART_DEV = 2
BLK = 21
ITERS = 2
P_SIZE = 128
OWNERS = 64
NBLK = 1344
WIN = 8
GROUPS = 15
CAP = 2


def particle_order(key):
    return jax.random.permutation(jax.random.fold_in(key, 11), P_SIZE).astype(jnp.int32)


def draw_owner_of(key, part):
    return particle_order(key)


def draw_partners(key, part):
    ordering = particle_order(key)
    inverse = jnp.zeros((P_SIZE,), jnp.int32).at[ordering].set(jnp.arange(P_SIZE, dtype=jnp.int32))
    choices_count = GROUPS * CAP
    scores = (jax.random.randint(jax.random.fold_in(key, 12), (OWNERS, choices_count), 0, 1 << 20) + 1) * choices_count
    positions = jnp.arange(choices_count, dtype=jnp.int32)[None, :]
    scores = jnp.where(positions < CAP, positions, scores + positions)
    chosen = jnp.argsort(scores, axis=1)[:, :BLK].astype(jnp.int32)
    group_index = chosen // CAP
    signed_gap = jnp.where(group_index == 0, OWNERS // 2, jnp.where(group_index < WIN, group_index, -(group_index - WIN + 1)))
    shifts = jax.random.randint(jax.random.fold_in(key, 13), (OWNERS, GROUPS), 0, PART_DEV)
    local_row = (chosen % CAP + jnp.take_along_axis(shifts, group_index, axis=1)) % PART_DEV
    holders = jnp.arange(OWNERS, dtype=jnp.int32)[:, None]
    row_ids = (holders + signed_gap) % OWNERS * PART_DEV + local_row
    return inverse[row_ids].reshape(OWNERS * BLK).astype(jnp.int32)


def draw_live(key, part):
    counts = jax.random.randint(jax.random.fold_in(key, 14), (OWNERS,), 1, BLK + 1)
    fullest = jax.random.randint(jax.random.fold_in(key, 15), (), 0, OWNERS)
    return counts.at[fullest].set(BLK).astype(jnp.int32)


def place_ends(entries, key, least, high):
    place = [jax.random.randint(jax.random.fold_in(key, axis), (), 0, length) for axis, length in enumerate(entries.shape)]
    main_axis = entries.shape.index(max(entries.shape))
    beside = place[:main_axis] + [(place[main_axis] + 1) % entries.shape[main_axis]] + place[main_axis + 1:]
    return entries.at[tuple(place)].set(least).at[tuple(beside)].set(high)


def block_levels(key, extent, shards, least, high):
    def one(position, blocks):
        steps = jax.random.uniform(jax.random.fold_in(jax.random.fold_in(key, 6), position), (blocks,), jnp.float32, least / len(shards), high / len(shards))
        return jnp.repeat(jnp.exp(steps), extent[position] // blocks).reshape((-1,) + (1,) * (len(extent) - position - 1))

    gain = one(*shards[0])
    for cut in shards[1:]:
        gain = gain * one(*cut)
    return gain


def gaussian(stream_key, extent, width, most, split=(), kind=jnp.bfloat16):
    drawn = jax.random.normal(stream_key, extent, jnp.float32) * width
    if len(split) > 0:
        drawn = block_levels(stream_key, extent, split, -0.22, 0.18) * drawn
    return jnp.clip(drawn, min=-most, max=most).astype(kind)


def setup_inputs(seed: int = 0) -> dict:
    arg_keys = jax.random.split(jax.random.key(seed), 8)
    incident = gaussian(arg_keys[0], (P_SIZE, 2, K, L), 1.0, 6.0, ((0, 64), (3, 2)), jnp.float32)
    tmat = gaussian(arg_keys[1], (P_SIZE, 2, L, L), (2 * L) ** -0.5, 0.1875, ((0, 64), (2, 2)), jnp.float32)
    blocks = gaussian(arg_keys[2], (NBLK, 2, L, L), ((2 * L * BLK) ** -0.5), 0.09375, ((0, 64), (3, 2)), jnp.float32)
    block_rows = place_ends(jax.random.randint(arg_keys[3], (NBLK,), 0, PART_DEV), jax.random.fold_in(arg_keys[3], 1), 0, PART_DEV - 1).astype(jnp.int32)
    partners = draw_partners(jax.random.fold_in(arg_keys[7], 71), 0)
    live = draw_live(jax.random.fold_in(arg_keys[7], 71), 0)
    owner_of = draw_owner_of(jax.random.fold_in(arg_keys[7], 71), 0)
    return dict(incident=incident, tmat=tmat, blocks=blocks, block_rows=block_rows, partners=partners, live=live, owner_of=owner_of)


HIGHEST = lax.Precision.HIGHEST


def complex_rows(matrix, vectors):
    directions = vectors.shape[1]
    stacked = vectors.reshape(2 * directions, vectors.shape[2])
    real_part = jnp.einsum("km,lm->kl", stacked, matrix[0], precision=HIGHEST, preferred_element_type=jnp.float32)
    imag_part = jnp.einsum("km,lm->kl", stacked, matrix[1], precision=HIGHEST, preferred_element_type=jnp.float32)
    return jnp.stack((real_part[:directions] - imag_part[directions:], imag_part[:directions] + real_part[directions:]))


def complex_cols(matrix, vectors):
    directions = vectors.shape[1]
    stacked = vectors.reshape(2 * directions, vectors.shape[2])
    real_part = jnp.einsum("kl,lm->km", stacked, matrix[0], precision=HIGHEST, preferred_element_type=jnp.float32)
    imag_part = jnp.einsum("kl,lm->km", stacked, matrix[1], precision=HIGHEST, preferred_element_type=jnp.float32)
    return jnp.stack((real_part[:directions] - imag_part[directions:], imag_part[:directions] + real_part[directions:]))


def reference(incident, tmat, blocks, block_rows, partners, live, owner_of):
    apply_tmat = jax.vmap(complex_rows)
    scattered = apply_tmat(tmat, incident)
    exciting = incident
    for iteration in range(ITERS):
        def accumulate(totals, block_index, current=scattered):
            holder = block_index // BLK
            holder_row = (holder * PART_DEV + block_rows[block_index]).astype(jnp.int32)
            partner_row = owner_of[partners[block_index]].astype(jnp.int32)
            active = (block_index % BLK) < live[holder]
            one_block = blocks[block_index]
            forward = complex_rows(one_block, current[partner_row])
            backward = complex_cols(one_block, current[holder_row])
            totals = totals.at[holder_row].add(jnp.where(active, forward, jnp.zeros_like(forward)))
            totals = totals.at[partner_row].add(jnp.where(active, backward, jnp.zeros_like(backward)))
            return totals, None
        totals, unused = lax.scan(accumulate, jnp.zeros_like(incident), jnp.arange(NBLK, dtype=jnp.int32))
        exciting = incident + totals
        scattered = apply_tmat(tmat, exciting)
    return scattered, exciting
```

```python
import functools

import jax
import jax.numpy as jnp
from jax import lax
from jax.experimental import pallas as pl
from jax.experimental.pallas import tpu as pltpu
from jax.sharding import PartitionSpec as P

ITERS = 2
SLOTS = 21
STAGES = 4
ROWS = 64
HALF = 256
MESH = pl.DeviceIdType.MESH
F32 = jnp.float32
BF16 = jnp.bfloat16


def split(x):
    hi = x.astype(BF16)
    lo = (x - hi.astype(F32)).astype(BF16)
    return hi, lo


def turned(v):
    return jnp.concatenate([-v[ROWS // 2 :], v[: ROWS // 2]], axis=0)


def dot_nn(a, b):
    return lax.dot_general(a, b, (((1,), (0,)), ((), ())), preferred_element_type=F32)


def dot_nt(a, b):
    return lax.dot_general(a, b, (((1,), (1,)), ((), ())), preferred_element_type=F32)


def stacked_parts(v):
    hi, lo = split(v)
    return jnp.concatenate([hi, lo], axis=0)


def kernel(
    meta, incident, tmat, blocks, out_s, out_e,
    field_a, field_b, transit, give, result, from_x, line_sum, line_in, from_z, cross_sum, cross_in,
    pair_e, pair_h, pair_n, near, m_hi, m_lo, stage, t_hi, t_lo, wide,
    f_send, f_recv, g_send, g_recv, p_send, p_recv, stage_sem,
):
    me = lax.axis_index("owner")
    core = lax.axis_index("pair")
    z = lax.rem(me, 4)
    group = lax.div(me, 4)

    def along_z(j):
        return group * 4 + lax.rem(z + j, 4)

    def along_g(dg):
        return lax.rem(group + dg + 16, 16) * 4 + z

    def to_owner(owner):
        return {"owner": owner}

    other_core = {"pair": 1 - core}

    def remote(src, dst, ssem, rsem, dev):
        return pltpu.make_async_remote_copy(
            src_ref=src, dst_ref=dst, send_sem=ssem, recv_sem=rsem,
            device_id=dev, device_id_type=MESH,
        )

    def fetch_block(n):
        return pltpu.make_async_copy(
            blocks.at[n], stage.at[lax.rem(n, STAGES)], stage_sem.at[lax.rem(n, STAGES)]
        )

    for n in range(STAGES):
        pltpu.make_async_copy(blocks.at[n], stage.at[n], stage_sem.at[n]).start()

    barrier = pltpu.get_barrier_semaphore()
    partners = [along_z(j) for j in (1, 2, 3)] + [along_g(d) for d in (1, -1, 2, -2, 8)]
    for owner in partners:
        pl.semaphore_signal(barrier, inc=1, device_id=to_owner(owner), device_id_type=MESH)
    pl.semaphore_signal(barrier, inc=1, device_id=other_core, device_id_type=MESH)
    pl.semaphore_wait(barrier, 9)

    fields = (field_a, field_b)
    sends = []

    pair0 = remote(incident, pair_e.at[0], p_send.at[0], p_recv.at[0], other_core)
    pair0.start()
    sends.append(pair0)

    for p in range(2):
        for c in range(2):
            hi, lo = split(tmat[p, c])
            t_hi[p, c] = hi
            t_lo[p, c] = lo

    def whole(mine, theirs):
        return jnp.concatenate(
            [jnp.where(core == 0, mine, theirs), jnp.where(core == 0, theirs, mine)], axis=1
        )

    def apply_t(p, v):
        a = stacked_parts(v)
        b = stacked_parts(turned(v))
        big = dot_nt(a, t_hi[p, 0]) + dot_nt(b, t_hi[p, 1])
        small = dot_nt(a[:ROWS], t_lo[p, 0]) + dot_nt(b[:ROWS], t_lo[p, 1])
        return big[:ROWS] + big[ROWS:] + small

    pair0.wait_recv()
    for p in range(2):
        fields[0][16 * p] = apply_t(p, whole(incident[p], pair_e[0, p]))

    for it in range(ITERS):
        ns = [0]
        field = fields[it]

        def send_field(src, dst, recv_index, owner, it=it, ns=ns):
            k = ns[0]
            ns[0] += 1
            c = remote(src, dst, f_send.at[it, k], f_recv.at[it, recv_index], to_owner(owner))
            c.start()
            sends.append(c)

        def got_field(index, it=it, field=field):
            ref = field.at[index] if index < 32 else transit.at[it, index - 32]
            pltpu.make_async_copy(ref, ref, f_recv.at[it, index]).wait()

        def q0(kind, j):
            return kind * 4 + j

        def q1(kind, j):
            return 16 + j * 4 + kind

        halves = []
        for p in range(2):
            c = remote(
                field.at[16 * p], pair_h.at[it, p], p_send.at[3 + it * 2 + p],
                p_recv.at[3 + it * 2 + p], other_core,
            )
            c.start()
            sends.append(c)
            halves.append(c)
        own0 = field.at[0]
        own1 = field.at[16]
        for j in (1, 3, 2):
            send_field(own0, field.at[q0(0, 4 - j)], q0(0, 4 - j), along_z(j))
        for dg, kind in ((1, 2), (-1, 1)):
            send_field(own1, field.at[q1(kind, 0)], q1(kind, 0), along_g(dg))
        for dg, t in ((2, 1), (-2, 0)):
            send_field(own1, transit.at[it, t], 32 + t, along_g(dg))
        for dg, kind in ((1, 2), (-1, 1)):
            send_field(own0, field.at[q0(kind, 0)], q0(kind, 0), along_g(dg))
        for j in (1, 3, 2):
            send_field(own1, field.at[q1(0, 4 - j)], q1(0, 4 - j), along_z(j))
        send_field(own0, field.at[q0(3, 0)], q0(3, 0), along_g(8))
        send_field(own1, field.at[q1(3, 0)], q1(3, 0), along_g(8))

        for p in range(2):
            halves[p].wait_recv()
            v = whole(field[16 * p], pair_h[it, p])
            wide[p, :, : 2 * HALF] = stacked_parts(v)
            wide[p, :, 2 * HALF :] = stacked_parts(turned(v))

        def load_block(n):
            fetch_block(n).wait()
            for c in range(2):
                hi, lo = split(stage[lax.rem(n, STAGES), c])
                m_hi[n, c * 512 : (c + 1) * 512] = hi
                m_lo[n, c * 512 : (c + 1) * 512] = lo

            @pl.when(n + STAGES < SLOTS)
            def _():
                fetch_block(n + STAGES).start()

        def backward(n, carry, it=it):
            if it == 0:
                load_block(n)
            left = wide[meta[SLOTS + n]]
            big = dot_nn(left, m_hi[n])
            small = dot_nn(left[:ROWS], m_lo[n])
            result[n] = big[:ROWS] + big[ROWS:] + small
            return carry

        lax.fori_loop(0, 10, backward, 0)

        for j in (1, 3, 2):
            got_field(q0(0, j))
            line = field.at[q0(0, j)]
            for dg, kind in ((1, 2), (-1, 1)):
                send_field(line, field.at[q0(kind, j)], q0(kind, j), along_g(dg))
            above = lax.rem(z + j, 4) > z
            send_field(
                line, field.at[q0(3, j)], q0(3, j),
                jnp.where(above, along_g(2), along_g(-2)),
            )
        for kind in (1, 2):
            got_field(q1(kind, 0))
            for j in (1, 3, 2):
                send_field(
                    field.at[q1(kind, 0)], field.at[q1(kind, 4 - j)],
                    q1(kind, 4 - j), along_z(j),
                )
        got_field(32)
        got_field(33)
        for j in (1, 3, 2):
            above = lax.rem(z + j, 4) > z
            send_field(
                transit.at[it, jnp.where(above, 0, 1)], field.at[q1(3, 4 - j)],
                q1(3, 4 - j), along_z(j),
            )

        lax.fori_loop(10, SLOTS, backward, 0)

        def fill(k, carry, it=it):
            flag = meta[3 * SLOTS + 33 + k].astype(F32)
            give[it, k] = result[meta[3 * SLOTS + 1 + k]] * flag
            return carry

        lax.fori_loop(1, 32, fill, 0)

        ng = [0]

        def send_give(src, dst, recv_index, owner, it=it, ng=ng):
            k = ng[0]
            ng[0] += 1
            c = remote(src, dst, g_send.at[it, k], g_recv.at[it, recv_index], to_owner(owner))
            c.start()
            sends.append(c)

        def got_give(ref, index, it=it):
            pltpu.make_async_copy(ref, ref, g_recv.at[it, index]).wait()

        send_give(give.at[it, 4:8], from_x.at[it, 1], 1, along_g(1))
        send_give(give.at[it, 8:12], from_x.at[it, 0], 0, along_g(-1))
        for j in (1, 3, 2):
            send_give(give.at[it, pl.ds(16 + 4 * j, 4)], from_z.at[it, 4 - j], 6 + 4 - j, along_z(j))
        for j in (1, 2, 3):
            below = lax.rem(z + j, 4) < z
            send_give(
                give.at[it, q0(3, j)], from_x.at[it, 2, j], 2 + j,
                jnp.where(below, along_g(2), along_g(-2)),
            )
        send_give(give.at[it, q0(3, 0)], from_x.at[it, 2, 0], 2, along_g(8))
        send_give(give.at[it, q1(3, 0)], from_z.at[it, 0, 3], 6, along_g(8))

        for kind in range(4):
            for j in range(4):
                if kind == 0 and j == 0:
                    continue
                if not (kind == 0):
                    got_field(q0(kind, j))
                if not (j == 0 and kind in (1, 2)):
                    got_field(q1(kind, j))

        for h in range(2):
            for p in range(2):
                near[it, h, p] = jnp.zeros((ROWS, HALF), F32)

        def forward(n, carry, it=it, field=field):
            v = field[meta[n]]
            a = stacked_parts(v)
            b = stacked_parts(turned(v))
            big = dot_nt(a, m_hi[n, :512]) + dot_nt(b, m_hi[n, 512:])
            small = dot_nt(a[:ROWS], m_lo[n, :512]) + dot_nt(b[:ROWS], m_lo[n, 512:])
            out = big[:ROWS] + big[ROWS:] + small
            alive = meta[2 * SLOTS + n].astype(F32)
            second = alive * meta[SLOTS + n].astype(F32)
            first = alive - second
            for h in range(2):
                part = out[:, h * HALF : (h + 1) * HALF]
                near[it, h, 0] += part * first
                near[it, h, 1] += part * second
            return carry

        lax.fori_loop(0, 10, forward, 0)

        for k in range(2):
            got_give(from_x.at[it, k], k)
        for j in range(1, 4):
            got_give(from_x.at[it, 2, j], 2 + j)
            line_sum[it, j] = (
                give[it, q0(0, j)] + from_x[it, 0, j] + from_x[it, 1, j] + from_x[it, 2, j]
            )
        for j in (1, 3, 2):
            send_give(line_sum.at[it, j], line_in.at[it, 4 - j], 10 + 4 - j, along_z(j))
        for j in range(1, 4):
            got_give(from_z.at[it, j], 6 + j)
        for k, kind in ((0, 1), (1, 2)):
            cross_sum[it, k] = (
                give[it, q1(kind, 0)]
                + from_z[it, 1, kind] + from_z[it, 2, kind] + from_z[it, 3, kind]
            )
        up = jnp.zeros((ROWS, HALF), F32)
        down = jnp.zeros((ROWS, HALF), F32)
        for j in range(1, 4):
            term = from_z[it, j, 3]
            above = (lax.rem(z + j, 4) > z).astype(F32)
            up += term * above
            down += term * (1.0 - above)
        cross_sum[it, 2] = up
        cross_sum[it, 3] = down
        for k, dg in ((0, 1), (1, -1), (2, 2), (3, -2)):
            send_give(cross_sum.at[it, k], cross_in.at[it, k], 14 + k, along_g(dg))

        lax.fori_loop(10, SLOTS, forward, 0)

        c = remote(
            near.at[it, 1 - core], pair_n.at[it], p_send.at[7 + it], p_recv.at[7 + it], other_core
        )
        c.start()
        sends.append(c)

        got_give(from_x.at[it, 2, 0], 2)
        got_give(from_z.at[it, 0, 3], 6)
        for j in range(1, 4):
            got_give(line_in.at[it, j], 10 + j)
        for k in range(4):
            got_give(cross_in.at[it, k], 14 + k)
        c.wait_recv()
        returned0 = (
            from_x[it, 0, 0] + from_x[it, 1, 0] + from_x[it, 2, 0]
            + line_in[it, 1] + line_in[it, 2] + line_in[it, 3]
        )
        returned1 = (
            from_z[it, 1, 0] + from_z[it, 2, 0] + from_z[it, 3, 0] + from_z[it, 0, 3]
            + cross_in[it, 0] + cross_in[it, 1] + cross_in[it, 2] + cross_in[it, 3]
        )
        out_e[0] = incident[0] + near[it, core, 0] + pair_n[it, 0] + returned0
        out_e[1] = incident[1] + near[it, core, 1] + pair_n[it, 1] + returned1
        swap = remote(
            out_e, pair_e.at[1 + it], p_send.at[1 + it], p_recv.at[1 + it], other_core
        )
        swap.start()
        swap.wait()
        for p in range(2):
            after = apply_t(p, whole(out_e[p], pair_e[1 + it, p]))
            if it + 1 < ITERS:
                fields[it + 1][16 * p] = after
            else:
                out_s[p] = after

    for c in sends:
        c.wait_send()


def tables(block_rows, partners, live, owner_of):
    me = lax.axis_index("owner")
    z = me % 4
    group = me // 4
    mine = lax.dynamic_slice(partners, (me * SLOTS,), (SLOTS,))
    ids = jnp.arange(owner_of.shape[0], dtype=jnp.int32)
    rows = jnp.sum(jnp.where(mine[:, None] == ids[None, :], owner_of[None, :], 0), axis=1)
    owner = rows // 2
    j = (owner % 4 - z) % 4
    dg = (owner // 4 - group) % 16
    kind = jnp.where(dg == 0, 0, jnp.where(dg == 1, 1, jnp.where(dg == 15, 2, 3)))
    where_ = jnp.where(rows % 2 == 0, kind * 4 + j, 16 + j * 4 + kind)
    slots = jnp.arange(SLOTS, dtype=jnp.int32)
    alive = (slots < live[0]).astype(jnp.int32)
    hit = (where_[None, :] == jnp.arange(32, dtype=jnp.int32)[:, None]) & (alive[None, :] > 0)
    slot_of = jnp.sum(jnp.where(hit, slots[None, :], 0), axis=1)
    found = jnp.sum(hit.astype(jnp.int32), axis=1)
    pad = jnp.zeros((1,), jnp.int32)
    return jnp.concatenate([where_, block_rows, alive, pad, slot_of, found]).astype(jnp.int32)


def local(incident, tmat, blocks, block_rows, partners, live, owner_of):
    meta = tables(block_rows, partners, live, owner_of)
    inc = incident.reshape(2, ROWS, HALF)
    vm = lambda shape, dt=F32: pltpu.VMEM(shape, dt)
    h = (ROWS, HALF)
    sem = pltpu.SemaphoreType.DMA
    shape = jax.ShapeDtypeStruct((2, ROWS, HALF), F32)
    scattered, exciting = pl.pallas_call(
        kernel,
        out_shape=(shape, shape),
        in_specs=[
            pl.BlockSpec(memory_space=pltpu.SMEM),
            pl.BlockSpec(memory_space=pltpu.VMEM),
            pl.BlockSpec(memory_space=pltpu.VMEM),
            pl.BlockSpec(memory_space=pl.ANY),
        ],
        out_specs=(pl.BlockSpec(memory_space=pltpu.VMEM),) * 2,
        scratch_shapes=[
            vm((32,) + h), vm((32,) + h), vm((2, 2) + h), vm((2, 32) + h), vm((SLOTS,) + h),
            vm((2, 3, 4) + h), vm((2, 4) + h), vm((2, 4) + h), vm((2, 4, 4) + h),
            vm((2, 4) + h), vm((2, 4) + h),
            vm((3, 2) + h), vm((2, 2) + h), vm((2, 2) + h), vm((2, 2, 2) + h),
            vm((SLOTS, 1024, HALF), BF16), vm((SLOTS, 1024, HALF), BF16),
            vm((STAGES, 2, 512, HALF)),
            vm((2, 2, HALF, 512), BF16), vm((2, 2, HALF, 512), BF16),
            vm((2, 2 * ROWS, 1024), BF16),
            sem((2, 32)), sem((2, 34)), sem((2, 17)), sem((2, 18)), sem((9,)), sem((9,)),
            sem((STAGES,)),
        ],
        compiler_params=pltpu.CompilerParams(
            collective_id=0, has_side_effects=True, vmem_limit_bytes=60 * 1024 * 1024
        ),
        name="scatter_steps",
    )(meta, inc, tmat, blocks)
    full = (2, 2, ROWS // 2, HALF)
    return scattered.reshape(full), exciting.reshape(full)


def solution(mesh):
    in_specs = (
        P("owner", None, None, "pair"),
        P("owner", None, "pair", None),
        P("owner", None, None, "pair"),
        P("owner"),
        P(),
        P("owner"),
        P(),
    )
    out_specs = (P("owner", None, None, "pair"), P("owner", None, None, "pair"))
    return jax.shard_map(local, mesh=mesh, in_specs=in_specs, out_specs=out_specs, check_vma=False)
```

```python
import functools

import jax
import jax.numpy as jnp
from jax import lax
from jax.experimental import pallas as pl
from jax.experimental.pallas import tpu as pltpu
from jax.sharding import PartitionSpec as P

ITERS = 2
SLOTS = 21
STAGES = 4
ROWS = 64
HALF = 256
MESH = pl.DeviceIdType.MESH
F32 = jnp.float32
BF16 = jnp.bfloat16


def split(x):
    hi = x.astype(BF16)
    lo = (x - hi.astype(F32)).astype(BF16)
    return hi, lo


def turned(v):
    return jnp.concatenate([-v[ROWS // 2 :], v[: ROWS // 2]], axis=0)


def dot_nn(a, b):
    return lax.dot_general(a, b, (((1,), (0,)), ((), ())), preferred_element_type=F32)


def dot_nt(a, b):
    return lax.dot_general(a, b, (((1,), (1,)), ((), ())), preferred_element_type=F32)


def stacked_parts(v):
    hi, lo = split(v)
    return jnp.concatenate([hi, lo], axis=0)


def kernel(
    partners_ref, owner_ref, rows_ref, live_ref, incident, tmat, blocks, out_s, out_e,
    field_a, field_b, transit, through_f, through_g, give, result, from_x, line_sum, line_in, from_z, cross_sum, cross_in,
    pair_e, pair_h, pair_n, near, m_hi, m_lo, stage, t_raw, t_hi, t_lo, wide,
    place, key, slot_of, found, f_send, f_recv, g_send, g_recv, p_send, p_recv, stage_sem, t_sem,
):
    me = lax.axis_index("owner")
    core = lax.axis_index("pair")
    z = lax.rem(me, 4)
    group = lax.div(me, 4)

    def along_z(j):
        return group * 4 + lax.rem(z + j, 4)

    def along_g(dg):
        return lax.rem(group + dg + 16, 16) * 4 + z

    x = lax.rem(group, 4)
    y = lax.div(group, 4)
    y_way = jnp.where(x < 2, 3, 1)
    even = lax.rem(z, 2) == 0

    def along_y(dy):
        return (lax.rem(y + dy, 4) * 4 + x) * 4 + z

    def to_owner(owner):
        return {"owner": owner}

    other_core = {"pair": 1 - core}

    def remote(src, dst, ssem, rsem, dev):
        return pltpu.make_async_remote_copy(
            src_ref=src, dst_ref=dst, send_sem=ssem, recv_sem=rsem,
            device_id=dev, device_id_type=MESH,
        )

    def fetch_block(n):
        return pltpu.make_async_copy(
            blocks.at[n], stage.at[lax.rem(n, STAGES)], stage_sem.at[lax.rem(n, STAGES)]
        )

    barrier = pltpu.get_barrier_semaphore()
    partners = [along_z(j) for j in (1, 2, 3)] + [along_g(d) for d in (1, -1, 2, -2)]
    partners += [along_y(1), along_y(3)]
    pl.semaphore_signal(barrier, inc=1, device_id=other_core, device_id_type=MESH)
    for owner in partners:
        pl.semaphore_signal(barrier, inc=1, device_id=to_owner(owner), device_id_type=MESH)

    t_copy = pltpu.make_async_copy(tmat, t_raw, t_sem.at[0])
    t_copy.start()
    for n in range(STAGES):
        pltpu.make_async_copy(blocks.at[n], stage.at[n], stage_sem.at[n]).start()

    def find(n, carry):
        row = owner_ref[partners_ref[me * SLOTS + n]]
        owner = lax.div(row, 2)
        j = lax.rem(lax.rem(owner, 4) - z + 4, 4)
        dg = lax.rem(lax.div(owner, 4) - group + 16, 16)
        kind = jnp.where(dg == 0, 0, jnp.where(dg == 1, 1, jnp.where(dg == 15, 2, 3)))
        which = lax.rem(row, 2)
        place[n] = (kind * 4 + j) * 2 + which
        at = jnp.where(which == 0, kind * 4 + j, 16 + j * 4 + kind)
        key[n] = jnp.where(n < live_ref[0], at, -1)
        return carry

    def invert(k, carry):
        slot = jnp.int32(0)
        flag = jnp.int32(0)
        for n in range(SLOTS):
            hit = key[n] == k
            slot = jnp.where(hit, n, slot)
            flag = jnp.where(hit, 1, flag)
        slot_of[k] = slot
        found[k] = flag
        return carry

    t_copy.wait()
    for p in range(2):
        for c in range(2):
            hi, lo = split(t_raw[p, c])
            t_hi[p, c] = hi
            t_lo[p, c] = lo

    pl.semaphore_wait(barrier, 10)

    fields = (field_a, field_b)
    sends = []

    pair0 = remote(incident, pair_e.at[0], p_send.at[0], p_recv.at[0], other_core)
    pair0.start()
    sends.append(pair0)

    def whole(mine, theirs):
        return jnp.concatenate(
            [jnp.where(core == 0, mine, theirs), jnp.where(core == 0, theirs, mine)], axis=1
        )

    def apply_t(p, v):
        a = stacked_parts(v)
        b = stacked_parts(turned(v))
        big = dot_nt(a, t_hi[p, 0]) + dot_nt(b, t_hi[p, 1])
        small = dot_nt(a[:ROWS], t_lo[p, 0]) + dot_nt(b[:ROWS], t_lo[p, 1])
        return big[:ROWS] + big[ROWS:] + small

    lax.fori_loop(0, SLOTS, find, 0)
    pair0.wait_recv()
    for p in range(2):
        fields[0][p] = apply_t(p, whole(incident[p], pair_e[0, p]))

    for it in range(ITERS):
        ns = [0]
        field = fields[it]

        def send_field(src, dst, recv_index, owner, it=it, ns=ns):
            k = ns[0]
            ns[0] += 1
            c = remote(src, dst, f_send.at[it, k], f_recv.at[it, recv_index], to_owner(owner))
            c.start()
            sends.append(c)

        def q0(kind, j):
            return kind * 4 + j

        def q1(kind, j):
            return 16 + j * 4 + kind

        def at(kind, j, row=None, field=field):
            k = (kind * 4 + j) * 2
            return field.at[pl.ds(k, 2)] if row is None else field.at[k + row]

        def arrive(ref, index, it=it):
            pltpu.make_async_copy(ref, ref, f_recv.at[it, index]).wait()

        own_z = {1: 0, 3: 1, 2: 2}
        near_g = {1: 3, 2: 4}

        halves = []
        for p in range(2):
            c = remote(
                field.at[p], pair_h.at[it, p], p_send.at[3 + it * 2 + p],
                p_recv.at[3 + it * 2 + p], other_core,
            )
            c.start()
            sends.append(c)
            halves.append(c)
        own = at(0, 0)
        send_field(own, at(0, 3), 1, along_z(1))
        send_field(own, at(0, 1), 0, along_z(3))
        send_field(own, at(2, 0), 4, along_g(1))
        send_field(own, at(1, 0), 3, along_g(-1))
        send_field(own, through_f.at[it], 5, along_y(y_way))

        for p in range(2):
            halves[p].wait_recv()
            v = whole(field[p], pair_h[it, p])
            wide[p, :, : 2 * HALF] = stacked_parts(v)
            wide[p, :, 2 * HALF :] = stacked_parts(turned(v))

        def load_block(n):
            fetch_block(n).wait()
            for c in range(2):
                hi, lo = split(stage[lax.rem(n, STAGES), c])
                m_hi[n, c * 512 : (c + 1) * 512] = hi
                m_lo[n, c * 512 : (c + 1) * 512] = lo

            @pl.when(n + STAGES < SLOTS)
            def _():
                fetch_block(n + STAGES).start()

        def backward(n, carry, it=it):
            if it == 0:
                load_block(n)
            left = wide[rows_ref[n]]
            big = dot_nn(left, m_hi[n])
            small = dot_nn(left[:ROWS], m_lo[n])
            result[n] = big[:ROWS] + big[ROWS:] + small
            return carry

        lax.fori_loop(0, 9, backward, 0)
        if it == 0:
            lax.fori_loop(1, 32, invert, 0)

        for j in (1, 3):
            arrive(at(0, j), own_z[j])
        send_field(
            field.at[pl.ds(jnp.where(even, 2, 6), 2)], at(0, 2), 2,
            jnp.where(even, along_z(3), along_z(1)),
        )
        for kind, dg in ((1, 1), (2, -1)):
            arrive(at(kind, 0), near_g[kind])
            send_field(at(kind, 0), transit.at[it, kind - 1], 6 + kind, along_g(-dg))
            send_field(at(kind, 0, 1), at(kind, 3, 1), 8 + kind, along_z(1))
            send_field(at(kind, 0, 1), at(kind, 1, 1), 10 + kind, along_z(3))
        for j in (1, 3):
            send_field(at(0, j, 0), at(2, j, 0), 12 + j, along_g(1))
            send_field(at(0, j, 0), at(1, j, 0), 16 + j, along_g(-1))
        arrive(through_f.at[it], 5)
        send_field(through_f.at[it], at(3, 0), 6, along_y(y_way))

        lax.fori_loop(9, 14, backward, 0)

        arrive(at(0, 2), 2)
        send_field(at(0, 2), at(2, 2), 14, along_g(1))
        send_field(at(0, 2), at(1, 2), 18, along_g(-1))
        arrive(transit.at[it, 0], 7)
        arrive(transit.at[it, 1], 8)
        send_field(transit.at[it, jnp.where(z < 3, 0, 1)], at(3, 3), 21, along_z(1))
        send_field(transit.at[it, jnp.where(z == 0, 0, 1)], at(3, 1), 16, along_z(3))

        lax.fori_loop(14, 18, backward, 0)

        arrive(at(3, 3), 21)
        arrive(at(3, 1), 16)
        send_field(
            field.at[pl.ds(jnp.where(even, 30, 26), 2)], at(3, 2), 20,
            jnp.where(even, along_z(1), along_z(3)),
        )

        lax.fori_loop(18, SLOTS, backward, 0)

        def fill(k, carry, it=it):
            flag = found[k].astype(F32)
            give[it, k] = result[slot_of[k]] * flag
            return carry

        lax.fori_loop(1, 32, fill, 0)

        ng = [0]

        def send_give(src, dst, recv_index, owner, it=it, ng=ng):
            k = ng[0]
            ng[0] += 1
            c = remote(src, dst, g_send.at[it, k], g_recv.at[it, recv_index], to_owner(owner))
            c.start()
            sends.append(c)

        def got_give(ref, index, it=it):
            pltpu.make_async_copy(ref, ref, g_recv.at[it, index]).wait()

        send_give(give.at[it, 4:8], from_x.at[it, 1], 1, along_g(1))
        send_give(give.at[it, 8:12], from_x.at[it, 0], 0, along_g(-1))
        for j in (1, 3, 2):
            send_give(give.at[it, pl.ds(16 + 4 * j, 4)], from_z.at[it, 4 - j], 6 + 4 - j, along_z(j))
        for j in (1, 2, 3):
            below = lax.rem(z + j, 4) < z
            send_give(
                give.at[it, q0(3, j)], from_x.at[it, 2, j], 2 + j,
                jnp.where(below, along_g(2), along_g(-2)),
            )
        send_give(give.at[it, q0(3, 0)], through_g.at[it, 0], 18, along_y(y_way))
        send_give(give.at[it, q1(3, 0)], through_g.at[it, 1], 19, along_y(y_way))

        for kind in (1, 2):
            arrive(at(kind, 3, 1), 8 + kind)
            arrive(at(kind, 1, 1), 10 + kind)
        for kind, base in ((2, 12), (1, 16)):
            for j in (1, 3):
                arrive(at(kind, j, 0), base + j)
            arrive(at(kind, 2), base + 2)
        arrive(at(3, 0), 6)
        arrive(at(3, 2), 20)

        for h in range(2):
            for p in range(2):
                near[it, h, p] = jnp.zeros((ROWS, HALF), F32)

        def forward(n, carry, it=it, field=field):
            v = field[place[n]]
            a = stacked_parts(v)
            b = stacked_parts(turned(v))
            big = dot_nt(a, m_hi[n, :512]) + dot_nt(b, m_hi[n, 512:])
            small = dot_nt(a[:ROWS], m_lo[n, :512]) + dot_nt(b[:ROWS], m_lo[n, 512:])
            out = big[:ROWS] + big[ROWS:] + small
            alive = (n < live_ref[0]).astype(F32)
            second = alive * rows_ref[n].astype(F32)
            first = alive - second
            for h in range(2):
                part = out[:, h * HALF : (h + 1) * HALF]
                near[it, h, 0] += part * first
                near[it, h, 1] += part * second
            return carry

        lax.fori_loop(0, SLOTS, forward, 0)

        c = remote(
            near.at[it, 1 - core], pair_n.at[it], p_send.at[7 + it], p_recv.at[7 + it], other_core
        )
        c.start()
        sends.append(c)

        got_give(through_g.at[it, 0], 18)
        send_give(through_g.at[it, 0], from_x.at[it, 2, 0], 2, along_y(y_way))
        got_give(through_g.at[it, 1], 19)
        send_give(through_g.at[it, 1], from_z.at[it, 0, 3], 6, along_y(y_way))
        for k in range(2):
            got_give(from_x.at[it, k], k)
        for j in range(1, 4):
            got_give(from_x.at[it, 2, j], 2 + j)
            line_sum[it, j] = (
                give[it, q0(0, j)] + from_x[it, 0, j] + from_x[it, 1, j] + from_x[it, 2, j]
            )
        for j in (1, 3, 2):
            send_give(line_sum.at[it, j], line_in.at[it, 4 - j], 10 + 4 - j, along_z(j))
        for j in range(1, 4):
            got_give(from_z.at[it, j], 6 + j)
        for k, kind in ((0, 1), (1, 2)):
            cross_sum[it, k] = (
                give[it, q1(kind, 0)]
                + from_z[it, 1, kind] + from_z[it, 2, kind] + from_z[it, 3, kind]
            )
        up = jnp.zeros((ROWS, HALF), F32)
        down = jnp.zeros((ROWS, HALF), F32)
        for j in range(1, 4):
            term = from_z[it, j, 3]
            above = (lax.rem(z + j, 4) > z).astype(F32)
            up += term * above
            down += term * (1.0 - above)
        cross_sum[it, 2] = up
        cross_sum[it, 3] = down
        for k, dg in ((0, 1), (1, -1), (2, 2), (3, -2)):
            send_give(cross_sum.at[it, k], cross_in.at[it, k], 14 + k, along_g(dg))

        got_give(from_x.at[it, 2, 0], 2)
        got_give(from_z.at[it, 0, 3], 6)
        for j in range(1, 4):
            got_give(line_in.at[it, j], 10 + j)
        for k in range(4):
            got_give(cross_in.at[it, k], 14 + k)
        c.wait_recv()
        returned0 = (
            from_x[it, 0, 0] + from_x[it, 1, 0] + from_x[it, 2, 0]
            + line_in[it, 1] + line_in[it, 2] + line_in[it, 3]
        )
        returned1 = (
            from_z[it, 1, 0] + from_z[it, 2, 0] + from_z[it, 3, 0] + from_z[it, 0, 3]
            + cross_in[it, 0] + cross_in[it, 1] + cross_in[it, 2] + cross_in[it, 3]
        )
        out_e[0] = incident[0] + near[it, core, 0] + pair_n[it, 0] + returned0
        out_e[1] = incident[1] + near[it, core, 1] + pair_n[it, 1] + returned1
        swap = remote(
            out_e, pair_e.at[1 + it], p_send.at[1 + it], p_recv.at[1 + it], other_core
        )
        swap.start()
        swap.wait()
        for p in range(2):
            after = apply_t(p, whole(out_e[p], pair_e[1 + it, p]))
            if it + 1 < ITERS:
                fields[it + 1][p] = after
            else:
                out_s[p] = after

    for c in sends:
        c.wait_send()


def settle(s_in, e_in, s_out, e_out):
    s_out[...] = s_in[...]
    e_out[...] = e_in[...]


def local(incident, tmat, blocks, block_rows, partners, live, owner_of):
    inc = incident.reshape(2, ROWS, HALF)
    vm = lambda shape, dt=F32: pltpu.VMEM(shape, dt)
    h = (ROWS, HALF)
    sem = pltpu.SemaphoreType.DMA
    shape = jax.ShapeDtypeStruct((2, ROWS, HALF), F32)
    scattered, exciting = pl.pallas_call(
        kernel,
        out_shape=(shape, shape),
        in_specs=[
            pl.BlockSpec(memory_space=pltpu.SMEM),
            pl.BlockSpec(memory_space=pltpu.SMEM),
            pl.BlockSpec(memory_space=pltpu.SMEM),
            pl.BlockSpec(memory_space=pltpu.SMEM),
            pl.BlockSpec(memory_space=pltpu.VMEM),
            pl.BlockSpec(memory_space=pl.ANY),
            pl.BlockSpec(memory_space=pl.ANY),
        ],
        out_specs=(pl.BlockSpec(memory_space=pltpu.VMEM),) * 2,
        scratch_shapes=[
            vm((32,) + h), vm((32,) + h), vm((2, 2, 2) + h), vm((2, 2) + h), vm((2, 2) + h), vm((2, 32) + h), vm((SLOTS,) + h),
            vm((2, 3, 4) + h), vm((2, 4) + h), vm((2, 4) + h), vm((2, 4, 4) + h),
            vm((2, 4) + h), vm((2, 4) + h),
            vm((3, 2) + h), vm((2, 2) + h), vm((2, 2) + h), vm((2, 2, 2) + h),
            vm((SLOTS, 1024, HALF), BF16), vm((SLOTS, 1024, HALF), BF16),
            vm((STAGES, 2, 512, HALF)),
            vm((2, 2, HALF, 512)), vm((2, 2, HALF, 512), BF16), vm((2, 2, HALF, 512), BF16),
            vm((2, 2 * ROWS, 1024), BF16),
            pltpu.SMEM((SLOTS,), jnp.int32), pltpu.SMEM((SLOTS,), jnp.int32),
            pltpu.SMEM((32,), jnp.int32), pltpu.SMEM((32,), jnp.int32),
            sem((2, 22)), sem((2, 22)), sem((2, 19)), sem((2, 20)), sem((9,)), sem((9,)),
            sem((STAGES,)), sem((1,)),
        ],
        compiler_params=pltpu.CompilerParams(
            collective_id=0, has_side_effects=True, vmem_limit_bytes=60 * 1024 * 1024
        ),
        name="scatter_steps",
    )(partners, owner_of, block_rows, live, inc, tmat, blocks)
    scattered, exciting = pl.pallas_call(settle, out_shape=(shape, shape), name="settle")(
        scattered, exciting
    )
    full = (2, 2, ROWS // 2, HALF)
    return scattered.reshape(full), exciting.reshape(full)


def solution(mesh):
    in_specs = (
        P("owner", None, None, "pair"),
        P("owner", None, "pair", None),
        P("owner", None, None, "pair"),
        P("owner"),
        P(),
        P("owner"),
        P(),
    )
    out_specs = (P("owner", None, None, "pair"), P("owner", None, None, "pair"))
    return jax.shard_map(local, mesh=mesh, in_specs=in_specs, out_specs=out_specs, check_vma=False)
```

```python
import functools

import jax
import jax.numpy as jnp
from jax import lax
from jax.experimental import pallas as pl
from jax.experimental.pallas import tpu as pltpu
from jax.sharding import PartitionSpec as P

ITERS = 2
SLOTS = 21
STAGES = 4
ROWS = 64
HALF = 256
MESH = pl.DeviceIdType.MESH
F32 = jnp.float32
BF16 = jnp.bfloat16


def split(x):
    hi = x.astype(BF16)
    lo = (x - hi.astype(F32)).astype(BF16)
    return hi, lo


def turned(v):
    return jnp.concatenate([-v[ROWS // 2 :], v[: ROWS // 2]], axis=0)


def dot_nn(a, b):
    return lax.dot_general(a, b, (((1,), (0,)), ((), ())), preferred_element_type=F32)


def dot_nt(a, b):
    return lax.dot_general(a, b, (((1,), (1,)), ((), ())), preferred_element_type=F32)


def stacked_parts(v):
    hi, lo = split(v)
    return jnp.concatenate([hi, lo], axis=0)


def kernel(
    partners_ref, owner_ref, rows_ref, live_ref, incident, tmat, blocks, out_s, out_e,
    field_a, field_b, transit, through_f, through_g, give, result, from_x, line_sum, line_in, from_z, cross_sum, cross_in,
    pair_e, pair_h, pair_n, near, m_hi, m_lo, stage, t_raw, t_hi, t_lo, wide,
    place, key, slot_of, found, f_send, f_recv, g_send, g_recv, p_send, p_recv, stage_sem, t_sem,
):
    me = lax.axis_index("owner")
    core = lax.axis_index("pair")
    z = lax.rem(me, 4)
    group = lax.div(me, 4)

    def along_z(j):
        return group * 4 + lax.rem(z + j, 4)

    def along_g(dg):
        return lax.rem(group + dg + 16, 16) * 4 + z

    x = lax.rem(group, 4)
    y = lax.div(group, 4)
    y_way = jnp.where(x < 2, 3, 1)
    even = lax.rem(z, 2) == 0

    def along_y(dy):
        return (lax.rem(y + dy, 4) * 4 + x) * 4 + z

    def to_owner(owner):
        return {"owner": owner}

    other_core = {"pair": 1 - core}

    def remote(src, dst, ssem, rsem, dev):
        return pltpu.make_async_remote_copy(
            src_ref=src, dst_ref=dst, send_sem=ssem, recv_sem=rsem,
            device_id=dev, device_id_type=MESH,
        )

    def fetch_block(n):
        return pltpu.make_async_copy(
            blocks.at[n], stage.at[lax.rem(n, STAGES)], stage_sem.at[lax.rem(n, STAGES)]
        )

    barrier = pltpu.get_barrier_semaphore()
    partners = [along_z(j) for j in (1, 2, 3)] + [along_g(d) for d in (1, -1, 2, -2)]
    partners += [along_y(1), along_y(3)]
    pl.semaphore_signal(barrier, inc=1, device_id=other_core, device_id_type=MESH)
    for owner in partners:
        pl.semaphore_signal(barrier, inc=1, device_id=to_owner(owner), device_id_type=MESH)

    t_copy = pltpu.make_async_copy(tmat, t_raw, t_sem.at[0])
    t_copy.start()
    def find(n, carry):
        row = owner_ref[partners_ref[me * SLOTS + n]]
        owner = lax.div(row, 2)
        j = lax.rem(lax.rem(owner, 4) - z + 4, 4)
        dg = lax.rem(lax.div(owner, 4) - group + 16, 16)
        kind = jnp.where(dg == 0, 0, jnp.where(dg == 1, 1, jnp.where(dg == 15, 2, 3)))
        which = lax.rem(row, 2)
        at = jnp.where(which == 0, kind * 4 + j, 16 + j * 4 + kind)
        place[n] = at
        key[n] = jnp.where(n < live_ref[0], at, -1)
        return carry

    def invert(k, carry):
        slot = jnp.int32(0)
        flag = jnp.int32(0)
        for n in range(SLOTS):
            hit = key[n] == k
            slot = jnp.where(hit, n, slot)
            flag = jnp.where(hit, 1, flag)
        slot_of[k] = slot
        found[k] = flag
        return carry

    t_copy.wait()
    for n in range(STAGES):
        pltpu.make_async_copy(blocks.at[n], stage.at[n], stage_sem.at[n]).start()
    for p in range(2):
        for c in range(2):
            hi, lo = split(t_raw[p, c])
            t_hi[p, c] = hi
            t_lo[p, c] = lo

    pl.semaphore_wait(barrier, 10)

    fields = (field_a, field_b)
    sends = []

    pair0 = remote(incident, pair_e.at[0], p_send.at[0], p_recv.at[0], other_core)
    pair0.start()
    sends.append(pair0)

    def whole(mine, theirs):
        return jnp.concatenate(
            [jnp.where(core == 0, mine, theirs), jnp.where(core == 0, theirs, mine)], axis=1
        )

    def apply_t(p, v):
        a = stacked_parts(v)
        b = stacked_parts(turned(v))
        big = dot_nt(a, t_hi[p, 0]) + dot_nt(b, t_hi[p, 1])
        small = dot_nt(a[:ROWS], t_lo[p, 0]) + dot_nt(b[:ROWS], t_lo[p, 1])
        return big[:ROWS] + big[ROWS:] + small

    lax.fori_loop(0, SLOTS, find, 0)

    def q0(kind, j):
        return kind * 4 + j

    def q1(kind, j):
        return 16 + j * 4 + kind

    counts = {}
    halves = {}

    def send_field(it, src, dst, recv_index, owner):
        k = counts.get(it, 0)
        counts[it] = k + 1
        c = remote(src, dst, f_send.at[it, k], f_recv.at[it, recv_index], to_owner(owner))
        c.start()
        sends.append(c)

    def share(it, p):
        c = remote(
            fields[it].at[16 * p], pair_h.at[it, p], p_send.at[5 + it * 2 + p],
            p_recv.at[5 + it * 2 + p], other_core,
        )
        c.start()
        sends.append(c)
        halves[it, p] = c

    def send_first(it):
        f = fields[it]
        for j in (2, 1, 3):
            send_field(it, f.at[0], f.at[q0(0, 4 - j)], q0(0, 4 - j), along_z(j))
        share(it, 0)

    def send_second(it):
        f = fields[it]
        for dg, t in ((2, 1), (-2, 0)):
            send_field(it, f.at[16], transit.at[it, t], 32 + t, along_g(dg))
        for dg, kind in ((1, 2), (-1, 1)):
            send_field(it, f.at[16], f.at[q1(kind, 0)], q1(kind, 0), along_g(dg))
        share(it, 1)
        send_field(it, f.at[0], through_f.at[it, 0], 34, along_y(y_way))
        send_field(it, f.at[16], through_f.at[it, 1], 35, along_y(y_way))
        for dg, kind in ((1, 2), (-1, 1)):
            send_field(it, f.at[0], f.at[q0(kind, 0)], q0(kind, 0), along_g(dg))
        for j in (2, 1, 3):
            send_field(it, f.at[16], f.at[q1(0, 4 - j)], q1(0, 4 - j), along_z(j))

    starts = (send_first, send_second)
    pair0.wait_recv()
    for p in range(2):
        fields[0][16 * p] = apply_t(p, whole(incident[p], pair_e[0, p]))
        starts[p](0)

    for it in range(ITERS):
        field = fields[it]

        def got_field(index, it=it, field=field):
            ref = field.at[index] if index < 32 else transit.at[it, index - 32]
            pltpu.make_async_copy(ref, ref, f_recv.at[it, index]).wait()

        for p in range(2):
            halves[it, p].wait_recv()
            v = whole(field[16 * p], pair_h[it, p])
            wide[p, :, : 2 * HALF] = stacked_parts(v)
            wide[p, :, 2 * HALF :] = stacked_parts(turned(v))

        def load_block(n):
            fetch_block(n).wait()
            for c in range(2):
                hi, lo = split(stage[lax.rem(n, STAGES), c])
                m_hi[n, c * 512 : (c + 1) * 512] = hi
                m_lo[n, c * 512 : (c + 1) * 512] = lo

            @pl.when(n + STAGES < SLOTS)
            def _():
                fetch_block(n + STAGES).start()

        def backward(n, carry, it=it):
            if it == 0:
                load_block(n)
            left = wide[rows_ref[n]]
            big = dot_nn(left, m_hi[n])
            small = dot_nn(left[:ROWS], m_lo[n])
            result[n] = big[:ROWS] + big[ROWS:] + small
            return carry

        lax.fori_loop(0, 10, backward, 0)
        if it == 0:
            lax.fori_loop(1, 32, invert, 0)

        got_field(32)
        got_field(33)
        for j in (2, 1, 3):
            above = lax.rem(z + j, 4) > z
            send_field(
                it, transit.at[it, jnp.where(above, 0, 1)], field.at[q1(3, 4 - j)],
                q1(3, 4 - j), along_z(j),
            )
        for j in (1, 3, 2):
            got_field(q0(0, j))
            line = field.at[q0(0, j)]
            above = lax.rem(z + j, 4) > z
            send_field(
                it, line, field.at[q0(3, j)], q0(3, j),
                jnp.where(above, along_g(2), along_g(-2)),
            )
            for dg, kind in ((1, 2), (-1, 1)):
                send_field(it, line, field.at[q0(kind, j)], q0(kind, j), along_g(dg))
        for kind in (1, 2):
            got_field(q1(kind, 0))
            for j in (2, 1, 3):
                send_field(
                    it, field.at[q1(kind, 0)], field.at[q1(kind, 4 - j)],
                    q1(kind, 4 - j), along_z(j),
                )
        for p in range(2):
            pltpu.make_async_copy(
                through_f.at[it, p], through_f.at[it, p], f_recv.at[it, 34 + p]
            ).wait()
            there = (q0(3, 0), q1(3, 0))[p]
            send_field(it, through_f.at[it, p], field.at[there], there, along_y(y_way))

        lax.fori_loop(10, SLOTS, backward, 0)

        def fill(k, carry, it=it):
            flag = found[k].astype(F32)
            give[it, k] = result[slot_of[k]] * flag
            return carry

        lax.fori_loop(1, 32, fill, 0)

        ng = [0]

        def send_give(src, dst, recv_index, owner, it=it, ng=ng):
            k = ng[0]
            ng[0] += 1
            c = remote(src, dst, g_send.at[it, k], g_recv.at[it, recv_index], to_owner(owner))
            c.start()
            sends.append(c)

        def got_give(ref, index, it=it):
            pltpu.make_async_copy(ref, ref, g_recv.at[it, index]).wait()

        for j in (2, 1, 3):
            send_give(
                give.at[it, pl.ds(17 + 4 * j, 3)], from_z.at[it, 4 - j, pl.ds(1, 3)], 6 + 4 - j,
                along_z(j),
            )
        for j in (1, 2, 3):
            below = lax.rem(z + j, 4) < z
            send_give(
                give.at[it, q0(3, j)], from_x.at[it, 2, j], 2 + j,
                jnp.where(below, along_g(2), along_g(-2)),
            )
        send_give(give.at[it, 5:8], from_x.at[it, 1, pl.ds(1, 3)], 1, along_g(1))
        send_give(give.at[it, 9:12], from_x.at[it, 0, pl.ds(1, 3)], 0, along_g(-1))
        send_give(give.at[it, q0(3, 0)], through_g.at[it, 0], 18, along_y(y_way))
        send_give(give.at[it, q1(3, 0)], through_g.at[it, 1], 19, along_y(y_way))
        for j in (1, 3, 2):
            send_give(give.at[it, 16 + 4 * j], from_z.at[it, 4 - j, 0], 19 + 4 - j, along_z(j))
        send_give(give.at[it, 4], from_x.at[it, 1, 0], 24, along_g(1))
        send_give(give.at[it, 8], from_x.at[it, 0, 0], 23, along_g(-1))

        for kind in range(4):
            for j in range(4):
                if kind == 0 and j == 0:
                    continue
                if not (kind == 0):
                    got_field(q0(kind, j))
                if not (j == 0 and kind in (1, 2)):
                    got_field(q1(kind, j))

        for h in range(2):
            for p in range(2):
                near[it, h, p] = jnp.zeros((ROWS, HALF), F32)

        def forward(n, carry, it=it, field=field):
            v = field[place[n]]
            a = stacked_parts(v)
            b = stacked_parts(turned(v))
            big = dot_nt(a, m_hi[n, :512]) + dot_nt(b, m_hi[n, 512:])
            small = dot_nt(a[:ROWS], m_lo[n, :512]) + dot_nt(b[:ROWS], m_lo[n, 512:])
            out = big[:ROWS] + big[ROWS:] + small
            alive = (n < live_ref[0]).astype(F32)
            second = alive * rows_ref[n].astype(F32)
            first = alive - second
            for h in range(2):
                part = out[:, h * HALF : (h + 1) * HALF]
                near[it, h, 0] += part * first
                near[it, h, 1] += part * second
            return carry

        lax.fori_loop(0, 14, forward, 0)

        got_give(through_g.at[it, 0], 18)
        send_give(through_g.at[it, 0], from_x.at[it, 2, 0], 2, along_y(y_way))
        got_give(through_g.at[it, 1], 19)
        send_give(through_g.at[it, 1], from_z.at[it, 0, 3], 6, along_y(y_way))
        for k in range(2):
            got_give(from_x.at[it, k, pl.ds(1, 3)], k)
        for j in range(1, 4):
            got_give(from_x.at[it, 2, j], 2 + j)
            line_sum[it, j] = (
                give[it, q0(0, j)] + from_x[it, 0, j] + from_x[it, 1, j] + from_x[it, 2, j]
            )
        for j in (1, 3, 2):
            send_give(line_sum.at[it, j], line_in.at[it, 4 - j], 10 + 4 - j, along_z(j))
        for j in range(1, 4):
            got_give(from_z.at[it, j, pl.ds(1, 3)], 6 + j)
        for k, kind in ((0, 1), (1, 2)):
            cross_sum[it, k] = (
                give[it, q1(kind, 0)]
                + from_z[it, 1, kind] + from_z[it, 2, kind] + from_z[it, 3, kind]
            )
        up = jnp.zeros((ROWS, HALF), F32)
        down = jnp.zeros((ROWS, HALF), F32)
        for j in range(1, 4):
            term = from_z[it, j, 3]
            above = (lax.rem(z + j, 4) > z).astype(F32)
            up += term * above
            down += term * (1.0 - above)
        cross_sum[it, 2] = up
        cross_sum[it, 3] = down
        for k, dg in ((0, 1), (1, -1), (2, 2), (3, -2)):
            send_give(cross_sum.at[it, k], cross_in.at[it, k], 14 + k, along_g(dg))

        lax.fori_loop(14, SLOTS, forward, 0)

        c = remote(
            near.at[it, 1 - core], pair_n.at[it], p_send.at[9 + it], p_recv.at[9 + it], other_core
        )
        c.start()
        sends.append(c)

        c.wait_recv()
        swaps = []
        for p in range(2):
            if p == 0:
                got_give(from_x.at[it, 2, 0], 2)
                for k in range(2):
                    got_give(from_x.at[it, k, 0], 23 + k)
                for j in range(1, 4):
                    got_give(line_in.at[it, j], 10 + j)
                returned = (
                    from_x[it, 0, 0] + from_x[it, 1, 0] + from_x[it, 2, 0]
                    + line_in[it, 1] + line_in[it, 2] + line_in[it, 3]
                )
            else:
                got_give(from_z.at[it, 0, 3], 6)
                for j in range(1, 4):
                    got_give(from_z.at[it, j, 0], 19 + j)
                for k in range(4):
                    got_give(cross_in.at[it, k], 14 + k)
                returned = (
                    from_z[it, 1, 0] + from_z[it, 2, 0] + from_z[it, 3, 0] + from_z[it, 0, 3]
                    + cross_in[it, 0] + cross_in[it, 1] + cross_in[it, 2] + cross_in[it, 3]
                )
            out_e[p] = incident[p] + near[it, core, p] + pair_n[it, p] + returned
            swap = remote(
                out_e.at[p], pair_e.at[1 + it, p], p_send.at[1 + 2 * it + p],
                p_recv.at[1 + 2 * it + p], other_core,
            )
            swap.start()
            swaps.append(swap)
        for p in range(2):
            swaps[p].wait()
            after = apply_t(p, whole(out_e[p], pair_e[1 + it, p]))
            if it + 1 < ITERS:
                fields[it + 1][16 * p] = after
                starts[p](it + 1)
            else:
                out_s[p] = after

    for c in sends:
        c.wait_send()


def settle(s_in, e_in, s_out, e_out):
    s_out[...] = s_in[...]
    e_out[...] = e_in[...]


def local(incident, tmat, blocks, block_rows, partners, live, owner_of):
    inc = incident.reshape(2, ROWS, HALF)
    vm = lambda shape, dt=F32: pltpu.VMEM(shape, dt)
    h = (ROWS, HALF)
    sem = pltpu.SemaphoreType.DMA
    shape = jax.ShapeDtypeStruct((2, ROWS, HALF), F32)
    scattered, exciting = pl.pallas_call(
        kernel,
        out_shape=(shape, shape),
        in_specs=[
            pl.BlockSpec(memory_space=pltpu.SMEM),
            pl.BlockSpec(memory_space=pltpu.SMEM),
            pl.BlockSpec(memory_space=pltpu.SMEM),
            pl.BlockSpec(memory_space=pltpu.SMEM),
            pl.BlockSpec(memory_space=pltpu.VMEM),
            pl.BlockSpec(memory_space=pl.ANY),
            pl.BlockSpec(memory_space=pl.ANY),
        ],
        out_specs=(pl.BlockSpec(memory_space=pltpu.VMEM),) * 2,
        scratch_shapes=[
            vm((32,) + h), vm((32,) + h), vm((2, 2) + h), vm((2, 2) + h), vm((2, 2) + h), vm((2, 32) + h), vm((SLOTS,) + h),
            vm((2, 3, 4) + h), vm((2, 4) + h), vm((2, 4) + h), vm((2, 4, 4) + h),
            vm((2, 4) + h), vm((2, 4) + h),
            vm((3, 2) + h), vm((2, 2) + h), vm((2, 2) + h), vm((2, 2, 2) + h),
            vm((SLOTS, 1024, HALF), BF16), vm((SLOTS, 1024, HALF), BF16),
            vm((STAGES, 2, 512, HALF)),
            vm((2, 2, HALF, 512)), vm((2, 2, HALF, 512), BF16), vm((2, 2, HALF, 512), BF16),
            vm((2, 2 * ROWS, 1024), BF16),
            pltpu.SMEM((SLOTS,), jnp.int32), pltpu.SMEM((SLOTS,), jnp.int32),
            pltpu.SMEM((32,), jnp.int32), pltpu.SMEM((32,), jnp.int32),
            sem((2, 34)), sem((2, 36)), sem((2, 24)), sem((2, 25)), sem((11,)), sem((11,)),
            sem((STAGES,)), sem((1,)),
        ],
        compiler_params=pltpu.CompilerParams(
            collective_id=0, has_side_effects=True, vmem_limit_bytes=60 * 1024 * 1024
        ),
        name="scatter_steps",
    )(partners, owner_of, block_rows, live, inc, tmat, blocks)
    scattered, exciting = pl.pallas_call(settle, out_shape=(shape, shape), name="settle")(
        scattered, exciting
    )
    full = (2, 2, ROWS // 2, HALF)
    return scattered.reshape(full), exciting.reshape(full)


def solution(mesh):
    in_specs = (
        P("owner", None, None, "pair"),
        P("owner", None, "pair", None),
        P("owner", None, None, "pair"),
        P("owner"),
        P(),
        P("owner"),
        P(),
    )
    out_specs = (P("owner", None, None, "pair"), P("owner", None, None, "pair"))
    return jax.shard_map(local, mesh=mesh, in_specs=in_specs, out_specs=out_specs, check_vma=False)
```

```python
import functools

import jax
import jax.numpy as jnp
from jax import lax
from jax.experimental import pallas as pl
from jax.experimental.pallas import tpu as pltpu
from jax.sharding import PartitionSpec as P

ITERS = 2
SLOTS = 21
STAGES = 4
ROWS = 64
HALF = 256
MESH = pl.DeviceIdType.MESH
F32 = jnp.float32
BF16 = jnp.bfloat16


def split(x):
    hi = x.astype(BF16)
    lo = (x - hi.astype(F32)).astype(BF16)
    return hi, lo


def turned(v):
    return jnp.concatenate([-v[ROWS // 2 :], v[: ROWS // 2]], axis=0)


def dot_nn(a, b):
    return lax.dot_general(a, b, (((1,), (0,)), ((), ())), preferred_element_type=F32)


def dot_nt(a, b):
    return lax.dot_general(a, b, (((1,), (1,)), ((), ())), preferred_element_type=F32)


def stacked_parts(v):
    hi, lo = split(v)
    return jnp.concatenate([hi, lo], axis=0)


def kernel(
    partners_ref, owner_ref, rows_ref, live_ref, incident, tmat, blocks, out_s, out_e,
    field_a, field_b, transit, through_f, through_g, give, result, from_x, line_sum, line_in, from_z, cross_sum, cross_in,
    pair_e, pair_h, pair_n, near, m_hi, m_lo, stage, t_raw, t_hi, t_lo, wide,
    place, key, slot_of, found, f_send, f_recv, g_send, g_recv, p_send, p_recv, stage_sem, t_sem,
):
    me = lax.axis_index("owner")
    core = lax.axis_index("pair")
    z = lax.rem(me, 4)
    group = lax.div(me, 4)

    def along_z(j):
        return group * 4 + lax.rem(z + j, 4)

    def along_g(dg):
        return lax.rem(group + dg + 16, 16) * 4 + z

    x = lax.rem(group, 4)
    y = lax.div(group, 4)
    y_way = jnp.where(x < 2, 3, 1)
    even = lax.rem(z, 2) == 0

    def along_y(dy):
        return (lax.rem(y + dy, 4) * 4 + x) * 4 + z

    def to_owner(owner):
        return {"owner": owner}

    other_core = {"pair": 1 - core}

    def remote(src, dst, ssem, rsem, dev):
        return pltpu.make_async_remote_copy(
            src_ref=src, dst_ref=dst, send_sem=ssem, recv_sem=rsem,
            device_id=dev, device_id_type=MESH,
        )

    def fetch_block(n):
        return pltpu.make_async_copy(
            blocks.at[n], stage.at[lax.rem(n, STAGES)], stage_sem.at[lax.rem(n, STAGES)]
        )

    barrier = pltpu.get_barrier_semaphore()
    partners = [along_z(j) for j in (1, 2, 3)] + [along_g(d) for d in (1, -1, 2, -2)]
    partners += [along_y(1), along_y(3)]
    pl.semaphore_signal(barrier, inc=1, device_id=other_core, device_id_type=MESH)
    for owner in partners:
        pl.semaphore_signal(barrier, inc=1, device_id=to_owner(owner), device_id_type=MESH)

    t_copy = pltpu.make_async_copy(tmat, t_raw, t_sem.at[0])
    t_copy.start()
    def find(n, carry):
        row = owner_ref[partners_ref[me * SLOTS + n]]
        owner = lax.div(row, 2)
        j = lax.rem(lax.rem(owner, 4) - z + 4, 4)
        dg = lax.rem(lax.div(owner, 4) - group + 16, 16)
        kind = jnp.where(dg == 0, 0, jnp.where(dg == 1, 1, jnp.where(dg == 15, 2, 3)))
        which = lax.rem(row, 2)
        at = jnp.where(which == 0, kind * 4 + j, 16 + j * 4 + kind)
        place[n] = at
        key[n] = jnp.where(n < live_ref[0], at, -1)
        return carry

    def invert(k, carry):
        slot = jnp.int32(0)
        flag = jnp.int32(0)
        for n in range(SLOTS):
            hit = key[n] == k
            slot = jnp.where(hit, n, slot)
            flag = jnp.where(hit, 1, flag)
        slot_of[k] = slot
        found[k] = flag
        return carry

    t_copy.wait()
    for n in range(STAGES):
        pltpu.make_async_copy(blocks.at[n], stage.at[n], stage_sem.at[n]).start()
    for p in range(2):
        for c in range(2):
            hi, lo = split(t_raw[p, c])
            t_hi[p, c] = hi
            t_lo[p, c] = lo

    pl.semaphore_wait(barrier, 10)

    fields = (field_a, field_b)
    sends = []

    pair0 = remote(incident, pair_e.at[0], p_send.at[0], p_recv.at[0], other_core)
    pair0.start()
    sends.append(pair0)

    def whole(mine, theirs):
        return jnp.concatenate(
            [jnp.where(core == 0, mine, theirs), jnp.where(core == 0, theirs, mine)], axis=1
        )

    def apply_t(p, v):
        a = stacked_parts(v)
        b = stacked_parts(turned(v))
        big = dot_nt(a, t_hi[p, 0]) + dot_nt(b, t_hi[p, 1])
        small = dot_nt(a[:ROWS], t_lo[p, 0]) + dot_nt(b[:ROWS], t_lo[p, 1])
        return big[:ROWS] + big[ROWS:] + small

    lax.fori_loop(0, SLOTS, find, 0)

    def q0(kind, j):
        return kind * 4 + j

    def q1(kind, j):
        return 16 + j * 4 + kind

    counts = {}
    halves = {}

    def send_field(it, src, dst, recv_index, owner):
        k = counts.get(it, 0)
        counts[it] = k + 1
        c = remote(src, dst, f_send.at[it, k], f_recv.at[it, recv_index], to_owner(owner))
        c.start()
        sends.append(c)

    def share(it, p):
        c = remote(
            fields[it].at[16 * p], pair_h.at[it, p], p_send.at[5 + it * 2 + p],
            p_recv.at[5 + it * 2 + p], other_core,
        )
        c.start()
        sends.append(c)
        halves[it, p] = c

    def send_first(it):
        f = fields[it]
        for j in (1, 3, 2):
            send_field(it, f.at[0], f.at[q0(0, 4 - j)], q0(0, 4 - j), along_z(j))
        share(it, 0)

    def send_second(it):
        f = fields[it]
        for dg, kind in ((1, 2), (-1, 1)):
            send_field(it, f.at[16], f.at[q1(kind, 0)], q1(kind, 0), along_g(dg))
        for dg, t in ((2, 1), (-2, 0)):
            send_field(it, f.at[16], transit.at[it, t], 32 + t, along_g(dg))
        share(it, 1)
        send_field(it, f.at[0], through_f.at[it, 0], 34, along_y(y_way))
        send_field(it, f.at[16], through_f.at[it, 1], 35, along_y(y_way))
        for dg, kind in ((1, 2), (-1, 1)):
            send_field(it, f.at[0], f.at[q0(kind, 0)], q0(kind, 0), along_g(dg))
        for j in (2, 1, 3):
            send_field(it, f.at[16], f.at[q1(0, 4 - j)], q1(0, 4 - j), along_z(j))

    starts = (send_first, send_second)
    pair0.wait_recv()
    for p in range(2):
        fields[0][16 * p] = apply_t(p, whole(incident[p], pair_e[0, p]))
        starts[p](0)

    for it in range(ITERS):
        field = fields[it]

        def got_field(index, it=it, field=field):
            ref = field.at[index] if index < 32 else transit.at[it, index - 32]
            pltpu.make_async_copy(ref, ref, f_recv.at[it, index]).wait()

        for p in range(2):
            halves[it, p].wait_recv()
            v = whole(field[16 * p], pair_h[it, p])
            wide[p, :, : 2 * HALF] = stacked_parts(v)
            wide[p, :, 2 * HALF :] = stacked_parts(turned(v))

        def load_block(n):
            fetch_block(n).wait()
            for c in range(2):
                hi, lo = split(stage[lax.rem(n, STAGES), c])
                m_hi[n, c * 512 : (c + 1) * 512] = hi
                m_lo[n, c * 512 : (c + 1) * 512] = lo

            @pl.when(n + STAGES < SLOTS)
            def _():
                fetch_block(n + STAGES).start()

        def backward(n, carry, it=it):
            if it == 0:
                load_block(n)
            left = wide[rows_ref[n]]
            big = dot_nn(left, m_hi[n])
            small = dot_nn(left[:ROWS], m_lo[n])
            result[n] = big[:ROWS] + big[ROWS:] + small
            return carry

        def forward_line(j, it=it, field=field):
            line = field.at[q0(0, j)]
            for dg, kind in ((1, 2), (-1, 1)):
                send_field(it, line, field.at[q0(kind, j)], q0(kind, j), along_g(dg))
            above = lax.rem(z + j, 4) > z
            send_field(
                it, line, field.at[q0(3, j)], q0(3, j),
                jnp.where(above, along_g(2), along_g(-2)),
            )

        lax.fori_loop(0, 8, backward, 0)

        for j in (1, 3):
            got_field(q0(0, j))
            forward_line(j)
        for kind in (1, 2):
            got_field(q1(kind, 0))
            for j in (2, 1, 3):
                send_field(
                    it, field.at[q1(kind, 0)], field.at[q1(kind, 4 - j)], q1(kind, 4 - j),
                    along_z(j),
                )
        for p in range(2):
            pltpu.make_async_copy(
                through_f.at[it, p], through_f.at[it, p], f_recv.at[it, 34 + p]
            ).wait()
            there = (q0(3, 0), q1(3, 0))[p]
            send_field(it, through_f.at[it, p], field.at[there], there, along_y(y_way))
        if it == 0:
            lax.fori_loop(1, 32, invert, 0)

        lax.fori_loop(8, 13, backward, 0)

        got_field(32)
        got_field(33)
        for j in (2, 1, 3):
            above = lax.rem(z + j, 4) > z
            send_field(
                it, transit.at[it, jnp.where(above, 0, 1)], field.at[q1(3, 4 - j)],
                q1(3, 4 - j), along_z(j),
            )
        got_field(q0(0, 2))
        forward_line(2)

        lax.fori_loop(13, SLOTS, backward, 0)

        def fill(k, carry, it=it):
            flag = found[k].astype(F32)
            give[it, k] = result[slot_of[k]] * flag
            return carry

        lax.fori_loop(1, 32, fill, 0)

        ng = [0]

        def send_give(src, dst, recv_index, owner, it=it, ng=ng):
            k = ng[0]
            ng[0] += 1
            c = remote(src, dst, g_send.at[it, k], g_recv.at[it, recv_index], to_owner(owner))
            c.start()
            sends.append(c)

        def got_give(ref, index, it=it):
            pltpu.make_async_copy(ref, ref, g_recv.at[it, index]).wait()

        for j in (2, 1, 3):
            send_give(
                give.at[it, pl.ds(17 + 4 * j, 3)], from_z.at[it, 4 - j, pl.ds(1, 3)], 6 + 4 - j,
                along_z(j),
            )
        for j in (1, 2, 3):
            below = lax.rem(z + j, 4) < z
            send_give(
                give.at[it, q0(3, j)], from_x.at[it, 2, j], 2 + j,
                jnp.where(below, along_g(2), along_g(-2)),
            )
        send_give(give.at[it, 5:8], from_x.at[it, 1, pl.ds(1, 3)], 1, along_g(1))
        send_give(give.at[it, 9:12], from_x.at[it, 0, pl.ds(1, 3)], 0, along_g(-1))
        send_give(give.at[it, q0(3, 0)], through_g.at[it, 0], 18, along_y(y_way))
        send_give(give.at[it, q1(3, 0)], through_g.at[it, 1], 19, along_y(y_way))
        for j in (1, 3, 2):
            send_give(give.at[it, 16 + 4 * j], from_z.at[it, 4 - j, 0], 19 + 4 - j, along_z(j))
        send_give(give.at[it, 4], from_x.at[it, 1, 0], 24, along_g(1))
        send_give(give.at[it, 8], from_x.at[it, 0, 0], 23, along_g(-1))

        for kind in range(4):
            for j in range(4):
                if kind == 0 and j == 0:
                    continue
                if not (kind == 0):
                    got_field(q0(kind, j))
                if not (j == 0 and kind in (1, 2)):
                    got_field(q1(kind, j))

        for h in range(2):
            for p in range(2):
                near[it, h, p] = jnp.zeros((ROWS, HALF), F32)

        def forward(n, carry, it=it, field=field):
            v = field[place[n]]
            a = stacked_parts(v)
            b = stacked_parts(turned(v))
            big = dot_nt(a, m_hi[n, :512]) + dot_nt(b, m_hi[n, 512:])
            small = dot_nt(a[:ROWS], m_lo[n, :512]) + dot_nt(b[:ROWS], m_lo[n, 512:])
            out = big[:ROWS] + big[ROWS:] + small
            alive = (n < live_ref[0]).astype(F32)
            second = alive * rows_ref[n].astype(F32)
            first = alive - second
            for h in range(2):
                part = out[:, h * HALF : (h + 1) * HALF]
                near[it, h, 0] += part * first
                near[it, h, 1] += part * second
            return carry

        got_give(through_g.at[it, 0], 18)
        send_give(through_g.at[it, 0], from_x.at[it, 2, 0], 2, along_y(y_way))
        got_give(through_g.at[it, 1], 19)
        send_give(through_g.at[it, 1], from_z.at[it, 0, 3], 6, along_y(y_way))
        lax.fori_loop(0, 10, forward, 0)

        for k in range(2):
            got_give(from_x.at[it, k, pl.ds(1, 3)], k)
        for j in range(1, 4):
            got_give(from_x.at[it, 2, j], 2 + j)
            line_sum[it, j] = (
                give[it, q0(0, j)] + from_x[it, 0, j] + from_x[it, 1, j] + from_x[it, 2, j]
            )
        for j in (1, 3, 2):
            send_give(line_sum.at[it, j], line_in.at[it, 4 - j], 10 + 4 - j, along_z(j))
        for j in range(1, 4):
            got_give(from_z.at[it, j, pl.ds(1, 3)], 6 + j)
        for k, kind in ((0, 1), (1, 2)):
            cross_sum[it, k] = (
                give[it, q1(kind, 0)]
                + from_z[it, 1, kind] + from_z[it, 2, kind] + from_z[it, 3, kind]
            )
        up = jnp.zeros((ROWS, HALF), F32)
        down = jnp.zeros((ROWS, HALF), F32)
        for j in range(1, 4):
            term = from_z[it, j, 3]
            above = (lax.rem(z + j, 4) > z).astype(F32)
            up += term * above
            down += term * (1.0 - above)
        cross_sum[it, 2] = up
        cross_sum[it, 3] = down
        for k, dg in ((0, 1), (1, -1), (2, 2), (3, -2)):
            send_give(cross_sum.at[it, k], cross_in.at[it, k], 14 + k, along_g(dg))

        lax.fori_loop(10, SLOTS, forward, 0)

        c = remote(
            near.at[it, 1 - core], pair_n.at[it], p_send.at[9 + it], p_recv.at[9 + it], other_core
        )
        c.start()
        sends.append(c)

        c.wait_recv()
        swaps = []
        for p in range(2):
            if p == 0:
                got_give(from_x.at[it, 2, 0], 2)
                for k in range(2):
                    got_give(from_x.at[it, k, 0], 23 + k)
                for j in range(1, 4):
                    got_give(line_in.at[it, j], 10 + j)
                returned = (
                    from_x[it, 0, 0] + from_x[it, 1, 0] + from_x[it, 2, 0]
                    + line_in[it, 1] + line_in[it, 2] + line_in[it, 3]
                )
            else:
                got_give(from_z.at[it, 0, 3], 6)
                for j in range(1, 4):
                    got_give(from_z.at[it, j, 0], 19 + j)
                for k in range(4):
                    got_give(cross_in.at[it, k], 14 + k)
                returned = (
                    from_z[it, 1, 0] + from_z[it, 2, 0] + from_z[it, 3, 0] + from_z[it, 0, 3]
                    + cross_in[it, 0] + cross_in[it, 1] + cross_in[it, 2] + cross_in[it, 3]
                )
            out_e[p] = incident[p] + near[it, core, p] + pair_n[it, p] + returned
            swap = remote(
                out_e.at[p], pair_e.at[1 + it, p], p_send.at[1 + 2 * it + p],
                p_recv.at[1 + 2 * it + p], other_core,
            )
            swap.start()
            swaps.append(swap)
        for p in range(2):
            swaps[p].wait()
            after = apply_t(p, whole(out_e[p], pair_e[1 + it, p]))
            if it + 1 < ITERS:
                fields[it + 1][16 * p] = after
                starts[p](it + 1)
            else:
                out_s[p] = after

    for c in sends:
        c.wait_send()


def settle(s_in, e_in, s_out, e_out):
    s_out[...] = s_in[...]
    e_out[...] = e_in[...]


def local(incident, tmat, blocks, block_rows, partners, live, owner_of):
    inc = incident.reshape(2, ROWS, HALF)
    vm = lambda shape, dt=F32: pltpu.VMEM(shape, dt)
    h = (ROWS, HALF)
    sem = pltpu.SemaphoreType.DMA
    shape = jax.ShapeDtypeStruct((2, ROWS, HALF), F32)
    scattered, exciting = pl.pallas_call(
        kernel,
        out_shape=(shape, shape),
        in_specs=[
            pl.BlockSpec(memory_space=pltpu.SMEM),
            pl.BlockSpec(memory_space=pltpu.SMEM),
            pl.BlockSpec(memory_space=pltpu.SMEM),
            pl.BlockSpec(memory_space=pltpu.SMEM),
            pl.BlockSpec(memory_space=pltpu.VMEM),
            pl.BlockSpec(memory_space=pl.ANY),
            pl.BlockSpec(memory_space=pl.ANY),
        ],
        out_specs=(pl.BlockSpec(memory_space=pltpu.VMEM),) * 2,
        scratch_shapes=[
            vm((32,) + h), vm((32,) + h), vm((2, 2) + h), vm((2, 2) + h), vm((2, 2) + h), vm((2, 32) + h), vm((SLOTS,) + h),
            vm((2, 3, 4) + h), vm((2, 4) + h), vm((2, 4) + h), vm((2, 4, 4) + h),
            vm((2, 4) + h), vm((2, 4) + h),
            vm((3, 2) + h), vm((2, 2) + h), vm((2, 2) + h), vm((2, 2, 2) + h),
            vm((SLOTS, 1024, HALF), BF16), vm((SLOTS, 1024, HALF), BF16),
            vm((STAGES, 2, 512, HALF)),
            vm((2, 2, HALF, 512)), vm((2, 2, HALF, 512), BF16), vm((2, 2, HALF, 512), BF16),
            vm((2, 2 * ROWS, 1024), BF16),
            pltpu.SMEM((SLOTS,), jnp.int32), pltpu.SMEM((SLOTS,), jnp.int32),
            pltpu.SMEM((32,), jnp.int32), pltpu.SMEM((32,), jnp.int32),
            sem((2, 34)), sem((2, 36)), sem((2, 24)), sem((2, 25)), sem((11,)), sem((11,)),
            sem((STAGES,)), sem((1,)),
        ],
        compiler_params=pltpu.CompilerParams(
            collective_id=0, has_side_effects=True, vmem_limit_bytes=60 * 1024 * 1024
        ),
        name="scatter_steps",
    )(partners, owner_of, block_rows, live, inc, tmat, blocks)
    scattered, exciting = pl.pallas_call(settle, out_shape=(shape, shape), name="settle")(
        scattered, exciting
    )
    full = (2, 2, ROWS // 2, HALF)
    return scattered.reshape(full), exciting.reshape(full)


def solution(mesh):
    in_specs = (
        P("owner", None, None, "pair"),
        P("owner", None, "pair", None),
        P("owner", None, None, "pair"),
        P("owner"),
        P(),
        P("owner"),
        P(),
    )
    out_specs = (P("owner", None, None, "pair"), P("owner", None, None, "pair"))
    return jax.shard_map(local, mesh=mesh, in_specs=in_specs, out_specs=out_specs, check_vma=False)
```

```python
import functools

import jax
import jax.numpy as jnp
from jax import lax
from jax.experimental import pallas as pl
from jax.experimental.pallas import tpu as pltpu
from jax.sharding import PartitionSpec as P

ITERS = 2
SLOTS = 21
STAGES = 4
ROWS = 64
HALF = 256
MESH = pl.DeviceIdType.MESH
F32 = jnp.float32
BF16 = jnp.bfloat16


def split(x):
    hi = x.astype(BF16)
    lo = (x - hi.astype(F32)).astype(BF16)
    return hi, lo


def turned(v):
    return jnp.concatenate([-v[ROWS // 2 :], v[: ROWS // 2]], axis=0)


def dot_nn(a, b):
    return lax.dot_general(a, b, (((1,), (0,)), ((), ())), preferred_element_type=F32)


def dot_nt(a, b):
    return lax.dot_general(a, b, (((1,), (1,)), ((), ())), preferred_element_type=F32)


def stacked_parts(v):
    hi, lo = split(v)
    return jnp.concatenate([hi, lo], axis=0)


def kernel(
    partners_ref, owner_ref, rows_ref, live_ref, incident, tmat, blocks, out_s, out_e,
    field_a, field_b, transit, through_f, through_g, give, result, from_x, line_sum, line_in, from_z, cross_sum, cross_in,
    pair_e, pair_h, pair_n, near, m_hi, m_lo, stage, t_raw, t_hi, t_lo, wide,
    place, key, slot_of, found, f_send, f_recv, g_send, g_recv, p_send, p_recv, stage_sem, t_sem,
):
    me = lax.axis_index("owner")
    core = lax.axis_index("pair")
    z = lax.rem(me, 4)
    group = lax.div(me, 4)

    def along_z(j):
        return group * 4 + lax.rem(z + j, 4)

    def along_g(dg):
        return lax.rem(group + dg + 16, 16) * 4 + z

    x = lax.rem(group, 4)
    y = lax.div(group, 4)
    y_way = jnp.where(x < 2, 3, 1)
    even = lax.rem(z, 2) == 0

    def along_y(dy):
        return (lax.rem(y + dy, 4) * 4 + x) * 4 + z

    def to_owner(owner):
        return {"owner": owner}

    other_core = {"pair": 1 - core}

    def remote(src, dst, ssem, rsem, dev):
        return pltpu.make_async_remote_copy(
            src_ref=src, dst_ref=dst, send_sem=ssem, recv_sem=rsem,
            device_id=dev, device_id_type=MESH,
        )

    def fetch_block(n):
        return pltpu.make_async_copy(
            blocks.at[n], stage.at[lax.rem(n, STAGES)], stage_sem.at[lax.rem(n, STAGES)]
        )

    barrier = pltpu.get_barrier_semaphore()
    partners = [along_z(j) for j in (1, 2, 3)] + [along_g(d) for d in (1, -1, 2, -2)]
    partners += [along_y(1), along_y(3)]
    pl.semaphore_signal(barrier, inc=1, device_id=other_core, device_id_type=MESH)
    for owner in partners:
        pl.semaphore_signal(barrier, inc=1, device_id=to_owner(owner), device_id_type=MESH)

    t_copy = pltpu.make_async_copy(tmat, t_raw, t_sem.at[0])
    t_copy.start()
    def find(n, carry):
        row = owner_ref[partners_ref[me * SLOTS + n]]
        owner = lax.div(row, 2)
        j = lax.rem(lax.rem(owner, 4) - z + 4, 4)
        dg = lax.rem(lax.div(owner, 4) - group + 16, 16)
        kind = jnp.where(dg == 0, 0, jnp.where(dg == 1, 1, jnp.where(dg == 15, 2, 3)))
        which = lax.rem(row, 2)
        at = jnp.where(which == 0, kind * 4 + j, 16 + j * 4 + kind)
        place[n] = at
        key[n] = jnp.where(n < live_ref[0], at, -1)
        return carry

    def invert(k, carry):
        slot = jnp.int32(0)
        flag = jnp.int32(0)
        for n in range(SLOTS):
            hit = key[n] == k
            slot = jnp.where(hit, n, slot)
            flag = jnp.where(hit, 1, flag)
        slot_of[k] = slot
        found[k] = flag
        return carry

    t_copy.wait()
    for n in range(STAGES):
        pltpu.make_async_copy(blocks.at[n], stage.at[n], stage_sem.at[n]).start()
    for p in range(2):
        for c in range(2):
            hi, lo = split(t_raw[p, c])
            t_hi[p, c] = hi
            t_lo[p, c] = lo

    pl.semaphore_wait(barrier, 10)

    fields = (field_a, field_b)
    sends = []

    pair0 = remote(incident, pair_e.at[0], p_send.at[0], p_recv.at[0], other_core)
    pair0.start()
    sends.append(pair0)

    def whole(mine, theirs):
        return jnp.concatenate(
            [jnp.where(core == 0, mine, theirs), jnp.where(core == 0, theirs, mine)], axis=1
        )

    def apply_t(p, v):
        a = stacked_parts(v)
        b = stacked_parts(turned(v))
        big = dot_nt(a, t_hi[p, 0]) + dot_nt(b, t_hi[p, 1])
        small = dot_nt(a[:ROWS], t_lo[p, 0]) + dot_nt(b[:ROWS], t_lo[p, 1])
        return big[:ROWS] + big[ROWS:] + small

    lax.fori_loop(0, SLOTS, find, 0)

    def q0(kind, j):
        return kind * 4 + j

    def q1(kind, j):
        return 16 + j * 4 + kind

    counts = {}
    halves = {}

    def send_field(it, src, dst, recv_index, owner):
        k = counts.get(it, 0)
        counts[it] = k + 1
        c = remote(src, dst, f_send.at[it, k], f_recv.at[it, recv_index], to_owner(owner))
        c.start()
        sends.append(c)

    def share(it, p):
        c = remote(
            fields[it].at[16 * p], pair_h.at[it, p], p_send.at[5 + it * 2 + p],
            p_recv.at[5 + it * 2 + p], other_core,
        )
        c.start()
        sends.append(c)
        halves[it, p] = c

    def send_first(it):
        f = fields[it]
        for j in (1, 3, 2):
            send_field(it, f.at[0], f.at[q0(0, 4 - j)], q0(0, 4 - j), along_z(j))
        share(it, 0)

    def send_second(it):
        f = fields[it]
        for dg, kind in ((1, 2), (-1, 1)):
            send_field(it, f.at[16], f.at[q1(kind, 0)], q1(kind, 0), along_g(dg))
        for dg, t in ((2, 1), (-2, 0)):
            send_field(it, f.at[16], transit.at[it, t], 32 + t, along_g(dg))
        share(it, 1)
        send_field(it, f.at[0], through_f.at[it, 0], 34, along_y(y_way))
        send_field(it, f.at[16], through_f.at[it, 1], 35, along_y(y_way))
        for dg, kind in ((1, 2), (-1, 1)):
            send_field(it, f.at[0], f.at[q0(kind, 0)], q0(kind, 0), along_g(dg))
        for j in (2, 1, 3):
            send_field(it, f.at[16], f.at[q1(0, 4 - j)], q1(0, 4 - j), along_z(j))

    starts = (send_first, send_second)
    pair0.wait_recv()
    for p in range(2):
        fields[0][16 * p] = apply_t(p, whole(incident[p], pair_e[0, p]))
        starts[p](0)

    for it in range(ITERS):
        field = fields[it]

        def got_field(index, it=it, field=field):
            ref = field.at[index] if index < 32 else transit.at[it, index - 32]
            pltpu.make_async_copy(ref, ref, f_recv.at[it, index]).wait()

        for p in range(2):
            halves[it, p].wait_recv()
            v = whole(field[16 * p], pair_h[it, p])
            wide[p, :, : 2 * HALF] = stacked_parts(v)
            wide[p, :, 2 * HALF :] = stacked_parts(turned(v))

        def load_block(n):
            fetch_block(n).wait()
            for c in range(2):
                hi, lo = split(stage[lax.rem(n, STAGES), c])
                m_hi[n, c * 512 : (c + 1) * 512] = hi
                m_lo[n, c * 512 : (c + 1) * 512] = lo

            @pl.when(n + STAGES < SLOTS)
            def _():
                fetch_block(n + STAGES).start()

        def backward(n, carry, it=it):
            if it == 0:
                load_block(n)
            left = wide[rows_ref[n]]
            big = dot_nn(left, m_hi[n])
            small = dot_nn(left[:ROWS], m_lo[n])
            result[n] = big[:ROWS] + big[ROWS:] + small
            return carry

        def forward_line(j, it=it, field=field):
            line = field.at[q0(0, j)]
            for dg, kind in ((1, 2), (-1, 1)):
                send_field(it, line, field.at[q0(kind, j)], q0(kind, j), along_g(dg))
            above = lax.rem(z + j, 4) > z
            send_field(
                it, line, field.at[q0(3, j)], q0(3, j),
                jnp.where(above, along_g(2), along_g(-2)),
            )

        lax.fori_loop(0, 7, backward, 0)

        for j in (1, 3):
            got_field(q0(0, j))
            forward_line(j)
        for kind in (1, 2):
            got_field(q1(kind, 0))
            for j in (2, 1, 3):
                send_field(
                    it, field.at[q1(kind, 0)], field.at[q1(kind, 4 - j)], q1(kind, 4 - j),
                    along_z(j),
                )
        for p in range(2):
            pltpu.make_async_copy(
                through_f.at[it, p], through_f.at[it, p], f_recv.at[it, 34 + p]
            ).wait()
            there = (q0(3, 0), q1(3, 0))[p]
            send_field(it, through_f.at[it, p], field.at[there], there, along_y(y_way))
        if it == 0:
            lax.fori_loop(1, 32, invert, 0)

        lax.fori_loop(7, 11, backward, 0)

        got_field(32)
        got_field(33)
        for j in (2, 1, 3):
            above = lax.rem(z + j, 4) > z
            send_field(
                it, transit.at[it, jnp.where(above, 0, 1)], field.at[q1(3, 4 - j)],
                q1(3, 4 - j), along_z(j),
            )
        got_field(q0(0, 2))
        forward_line(2)

        lax.fori_loop(11, SLOTS, backward, 0)

        def fill(k, carry, it=it):
            flag = found[k].astype(F32)
            give[it, k] = result[slot_of[k]] * flag
            return carry

        lax.fori_loop(1, 32, fill, 0)

        ng = [0]

        def send_give(src, dst, recv_index, owner, it=it, ng=ng):
            k = ng[0]
            ng[0] += 1
            c = remote(src, dst, g_send.at[it, k], g_recv.at[it, recv_index], to_owner(owner))
            c.start()
            sends.append(c)

        def got_give(ref, index, it=it):
            pltpu.make_async_copy(ref, ref, g_recv.at[it, index]).wait()

        for j in (2, 1, 3):
            send_give(
                give.at[it, pl.ds(17 + 4 * j, 3)], from_z.at[it, 4 - j, pl.ds(1, 3)], 6 + 4 - j,
                along_z(j),
            )
        for j in (1, 2, 3):
            below = lax.rem(z + j, 4) < z
            send_give(
                give.at[it, q0(3, j)], from_x.at[it, 2, j], 2 + j,
                jnp.where(below, along_g(2), along_g(-2)),
            )
        send_give(give.at[it, 5:8], from_x.at[it, 1, pl.ds(1, 3)], 1, along_g(1))
        send_give(give.at[it, 9:12], from_x.at[it, 0, pl.ds(1, 3)], 0, along_g(-1))
        send_give(give.at[it, q0(3, 0)], through_g.at[it, 0], 18, along_y(y_way))
        send_give(give.at[it, q1(3, 0)], through_g.at[it, 1], 19, along_y(y_way))
        for j in (1, 3, 2):
            send_give(give.at[it, 16 + 4 * j], from_z.at[it, 4 - j, 0], 19 + 4 - j, along_z(j))
        send_give(give.at[it, 4], from_x.at[it, 1, 0], 24, along_g(1))
        send_give(give.at[it, 8], from_x.at[it, 0, 0], 23, along_g(-1))

        for kind in range(4):
            for j in range(4):
                if kind == 0 and j == 0:
                    continue
                if not (kind == 0):
                    got_field(q0(kind, j))
                if not (j == 0 and kind in (1, 2)):
                    got_field(q1(kind, j))

        for h in range(2):
            for p in range(2):
                near[it, h, p] = jnp.zeros((ROWS, HALF), F32)

        def forward(n, carry, it=it, field=field):
            v = field[place[n]]
            a = stacked_parts(v)
            b = stacked_parts(turned(v))
            big = dot_nt(a, m_hi[n, :512]) + dot_nt(b, m_hi[n, 512:])
            small = dot_nt(a[:ROWS], m_lo[n, :512]) + dot_nt(b[:ROWS], m_lo[n, 512:])
            out = big[:ROWS] + big[ROWS:] + small
            alive = (n < live_ref[0]).astype(F32)
            second = alive * rows_ref[n].astype(F32)
            first = alive - second
            for h in range(2):
                part = out[:, h * HALF : (h + 1) * HALF]
                near[it, h, 0] += part * first
                near[it, h, 1] += part * second
            return carry

        got_give(through_g.at[it, 0], 18)
        send_give(through_g.at[it, 0], from_x.at[it, 2, 0], 2, along_y(y_way))
        got_give(through_g.at[it, 1], 19)
        send_give(through_g.at[it, 1], from_z.at[it, 0, 3], 6, along_y(y_way))
        lax.fori_loop(0, 9, forward, 0)

        for k in range(2):
            got_give(from_x.at[it, k, pl.ds(1, 3)], k)
        for j in range(1, 4):
            got_give(from_x.at[it, 2, j], 2 + j)
            line_sum[it, j] = (
                give[it, q0(0, j)] + from_x[it, 0, j] + from_x[it, 1, j] + from_x[it, 2, j]
            )
        for j in (1, 3, 2):
            send_give(line_sum.at[it, j], line_in.at[it, 4 - j], 10 + 4 - j, along_z(j))
        for j in range(1, 4):
            got_give(from_z.at[it, j, pl.ds(1, 3)], 6 + j)
        for k, kind in ((0, 1), (1, 2)):
            cross_sum[it, k] = (
                give[it, q1(kind, 0)]
                + from_z[it, 1, kind] + from_z[it, 2, kind] + from_z[it, 3, kind]
            )
        up = jnp.zeros((ROWS, HALF), F32)
        down = jnp.zeros((ROWS, HALF), F32)
        for j in range(1, 4):
            term = from_z[it, j, 3]
            above = (lax.rem(z + j, 4) > z).astype(F32)
            up += term * above
            down += term * (1.0 - above)
        cross_sum[it, 2] = up
        cross_sum[it, 3] = down
        for k, dg in ((0, 1), (1, -1), (2, 2), (3, -2)):
            send_give(cross_sum.at[it, k], cross_in.at[it, k], 14 + k, along_g(dg))

        lax.fori_loop(9, SLOTS, forward, 0)

        c = remote(
            near.at[it, 1 - core], pair_n.at[it], p_send.at[9 + it], p_recv.at[9 + it], other_core
        )
        c.start()
        sends.append(c)

        c.wait_recv()
        swaps = []
        for p in range(2):
            if p == 0:
                got_give(from_x.at[it, 2, 0], 2)
                for k in range(2):
                    got_give(from_x.at[it, k, 0], 23 + k)
                for j in range(1, 4):
                    got_give(line_in.at[it, j], 10 + j)
                returned = (
                    from_x[it, 0, 0] + from_x[it, 1, 0] + from_x[it, 2, 0]
                    + line_in[it, 1] + line_in[it, 2] + line_in[it, 3]
                )
            else:
                got_give(from_z.at[it, 0, 3], 6)
                for j in range(1, 4):
                    got_give(from_z.at[it, j, 0], 19 + j)
                for k in range(4):
                    got_give(cross_in.at[it, k], 14 + k)
                returned = (
                    from_z[it, 1, 0] + from_z[it, 2, 0] + from_z[it, 3, 0] + from_z[it, 0, 3]
                    + cross_in[it, 0] + cross_in[it, 1] + cross_in[it, 2] + cross_in[it, 3]
                )
            out_e[p] = incident[p] + near[it, core, p] + pair_n[it, p] + returned
            swap = remote(
                out_e.at[p], pair_e.at[1 + it, p], p_send.at[1 + 2 * it + p],
                p_recv.at[1 + 2 * it + p], other_core,
            )
            swap.start()
            swaps.append(swap)
        for p in range(2):
            swaps[p].wait()
            after = apply_t(p, whole(out_e[p], pair_e[1 + it, p]))
            if it + 1 < ITERS:
                fields[it + 1][16 * p] = after
                starts[p](it + 1)
            else:
                out_s[p] = after

    for c in sends:
        c.wait_send()


def settle(s_in, e_in, s_out, e_out):
    s_out[...] = s_in[...]
    e_out[...] = e_in[...]


def local(incident, tmat, blocks, block_rows, partners, live, owner_of):
    inc = incident.reshape(2, ROWS, HALF)
    vm = lambda shape, dt=F32: pltpu.VMEM(shape, dt)
    h = (ROWS, HALF)
    sem = pltpu.SemaphoreType.DMA
    shape = jax.ShapeDtypeStruct((2, ROWS, HALF), F32)
    scattered, exciting = pl.pallas_call(
        kernel,
        out_shape=(shape, shape),
        in_specs=[
            pl.BlockSpec(memory_space=pltpu.SMEM),
            pl.BlockSpec(memory_space=pltpu.SMEM),
            pl.BlockSpec(memory_space=pltpu.SMEM),
            pl.BlockSpec(memory_space=pltpu.SMEM),
            pl.BlockSpec(memory_space=pltpu.VMEM),
            pl.BlockSpec(memory_space=pl.ANY),
            pl.BlockSpec(memory_space=pl.ANY),
        ],
        out_specs=(pl.BlockSpec(memory_space=pltpu.VMEM),) * 2,
        scratch_shapes=[
            vm((32,) + h), vm((32,) + h), vm((2, 2) + h), vm((2, 2) + h), vm((2, 2) + h), vm((2, 32) + h), vm((SLOTS,) + h),
            vm((2, 3, 4) + h), vm((2, 4) + h), vm((2, 4) + h), vm((2, 4, 4) + h),
            vm((2, 4) + h), vm((2, 4) + h),
            vm((3, 2) + h), vm((2, 2) + h), vm((2, 2) + h), vm((2, 2, 2) + h),
            vm((SLOTS, 1024, HALF), BF16), vm((SLOTS, 1024, HALF), BF16),
            vm((STAGES, 2, 512, HALF)),
            vm((2, 2, HALF, 512)), vm((2, 2, HALF, 512), BF16), vm((2, 2, HALF, 512), BF16),
            vm((2, 2 * ROWS, 1024), BF16),
            pltpu.SMEM((SLOTS,), jnp.int32), pltpu.SMEM((SLOTS,), jnp.int32),
            pltpu.SMEM((32,), jnp.int32), pltpu.SMEM((32,), jnp.int32),
            sem((2, 34)), sem((2, 36)), sem((2, 24)), sem((2, 25)), sem((11,)), sem((11,)),
            sem((STAGES,)), sem((1,)),
        ],
        compiler_params=pltpu.CompilerParams(
            collective_id=0, has_side_effects=True, vmem_limit_bytes=60 * 1024 * 1024
        ),
        name="scatter_steps",
    )(partners, owner_of, block_rows, live, inc, tmat, blocks)
    scattered, exciting = pl.pallas_call(settle, out_shape=(shape, shape), name="settle")(
        scattered, exciting
    )
    full = (2, 2, ROWS // 2, HALF)
    return scattered.reshape(full), exciting.reshape(full)


def solution(mesh):
    in_specs = (
        P("owner", None, None, "pair"),
        P("owner", None, "pair", None),
        P("owner", None, None, "pair"),
        P("owner"),
        P(),
        P("owner"),
        P(),
    )
    out_specs = (P("owner", None, None, "pair"), P("owner", None, None, "pair"))
    return jax.shard_map(local, mesh=mesh, in_specs=in_specs, out_specs=out_specs, check_vma=False)
```
